256 devices in a mesh: dp: 64 (over z_hi, y, x), mp: 4 (over z_lo, core).
Axes of the slice: x: 4, y: 4, z: 8 (z_hi: 4, z_lo: 2; z = z_hi * 2 + z_lo), core: 2. Of those that a mesh axis runs over, the one named last changes fastest.
Arguments:
- hidden: bfloat16 [2048, 16, 2048], P('dp', None, 'mp'), may hold values from -6 to 6
- norm_gain: bfloat16 [2048], P('mp'), may hold values from 0.099609375 to 1.8984375
- in_x: bfloat16 [2048, 4096], P('dp', 'mp'), may hold values from -0.125 to 0.125
- in_z: bfloat16 [2048, 4096], P('dp', 'mp'), may hold values from -0.125 to 0.125
- conv_weight: float32 [4, 4096], P(None, 'mp'), may hold values from -3 to 3
- conv_bias: float32 [4096], P('mp'), may hold values from -3 to 3
- x_proj: bfloat16 [4096, 160], P(('mp', 'dp')), may hold values from -0.09375 to 0.09375
- dt_proj: bfloat16 [128, 4096], P('dp', 'mp'), may hold values from -0.5 to 0.5
- dt_bias: float32 [4096], P('mp'), may hold values from -5 to -1
- a_log: float32 [16, 4096], P(None, 'mp'), may hold values from 0 to 2.77
- skip: float32 [4096], P('mp'), may hold values from 0.5 to 1.5
- out_proj: bfloat16 [4096, 2048], P('mp', 'dp'), may hold values from -0.09375 to 0.09375
- state_pool: float32 [2560, 16, 4096], P('dp', None, 'mp'), may hold values from -6 to 6
- conv_pool: float32 [2560, 3, 4096], P('dp', None, 'mp'), may hold values from -6 to 6
- permutation: int32 [2048], P('dp'), may hold values from 0 to 2047, as said below
- page_table: int32 [2048], P('dp'), may hold values from 0 to 2559, as said below
- accepted: int32 [2048], P('dp'), may hold values from 1 to 16
Outputs:
- verified: bfloat16 [2048, 16, 2048], P('dp', None, 'mp')
- new_state_pool: float32 [2560, 16, 4096], P('dp', None, 'mp')
- new_conv_pool: float32 [2560, 3, 4096], P('dp', None, 'mp')
The draws below stay inside these ranges and needn't reach their ends.
Inputs may be any that keep to these rules, and one draw needn't show every extreme that they name: `permutation`: A request at position j of the block of dp index d goes to position j of the block of dp index (d + o) mod 64, where the shift o depends only on j mod 32 and takes 32 different values; so each dp index sends exactly 1 request to each of 32 dp indices and receives 32. `page_table`: the requests of dp index d use distinct slots among the 40 slots d * 40 .. (d + 1) * 40 - 1.
All inputs are finite; a program needn't handle non-finite values.
Results may differ from the reference program's by a relative error of at most 0.0065.
Values may be sent and summed in bfloat16 or wider, within the bound.
No kernel may reach another device: no remote copies, remote signals or barrier semaphores. Data moves between devices by JAX's collectives and lax.ppermute only.
A program may use at most 128 MiB of HBM per device.

```python
import jax
import jax.numpy as jnp
from jax import lax

D = 2048
INNER = 4096
STATE = 16
RANK = 128
CONV = 4
DRAFTS = 16
REQ_DEV = 32
POOL_DEV = 40
REQUESTS = 2048
SLOTS = 2560
PEERS = 32
N_DP = 64


def draw_permutation(key, part):
    values = jnp.arange(N_DP, dtype=jnp.int32)
    scores = jax.random.permutation(jax.random.fold_in(key, 3), N_DP).astype(jnp.int32)
    scores = jnp.where(values == 1, -3, jnp.where(values == N_DP - 1, -2, jnp.where(values == N_DP // 2, -1, scores))).astype(jnp.int32)
    chosen = jnp.argsort(scores, stable=True)[:PEERS].astype(jnp.int32)
    mixing = jax.random.permutation(jax.random.fold_in(key, 5), PEERS).astype(jnp.int32)
    shifts = chosen[mixing]
    order = jnp.arange(REQUESTS, dtype=jnp.int32)
    source = order // REQ_DEV
    within = order % REQ_DEV
    target = (source + shifts[within % PEERS]) % N_DP
    return (target * REQ_DEV + within).astype(jnp.int32)


def draw_page_table(key, part):
    keys = jax.random.split(jax.random.fold_in(key, 7), N_DP)
    chosen = jax.vmap(lambda one_key: jax.random.permutation(one_key, POOL_DEV)[:REQ_DEV].astype(jnp.int32))(keys)
    offsets = (jnp.arange(N_DP, dtype=jnp.int32) * POOL_DEV)[:, None]
    return (chosen + offsets).reshape(REQUESTS).astype(jnp.int32)


def place_ends(entries, key, low, largest):
    longest = entries.shape.index(max(entries.shape))
    spots = []
    for shift in (0, 1):
        where = [jax.random.randint(jax.random.fold_in(key, axis), (), 0, length) for axis, length in enumerate(entries.shape)]
        where[longest] = (where[longest] + shift) % entries.shape[longest]
        spots.append(tuple(where))
    return entries.at[spots[0]].set(low).at[spots[1]].set(largest)


def block_levels(own_key, extent, shards, low, high):
    def one(position, parts):
        draws = jax.random.uniform(jax.random.fold_in(jax.random.fold_in(own_key, 6), position), (parts,), jnp.float32, low / len(shards), high / len(shards))
        return jnp.repeat(jnp.exp(draws), extent[position] // parts).reshape((-1,) + (1,) * (len(extent) - position - 1))

    factor_of = one(*shards[0])
    for cut in shards[1:]:
        factor_of = factor_of * one(*cut)
    return factor_of


def gaussian(own_key, extent, scale, most, pieces=(), kind=jnp.bfloat16):
    gain = block_levels(own_key, extent, pieces, -0.22, 0.18) if pieces else 1.0
    drawn = jax.random.normal(own_key, extent, jnp.float32) * scale * gain
    return jnp.minimum(jnp.maximum(drawn, -most), most).astype(kind)


def setup_inputs(seed: int = 0) -> dict:
    streams_of = jax.random.split(jax.random.key(seed), 18)
    return {
        "hidden": gaussian(streams_of[0], (REQUESTS, DRAFTS, D), 1.0, 6.0, ((0, 64), (2, 4))),
        "norm_gain": jnp.clip(1.0 + 0.18 * jax.random.normal(streams_of[1], (D,), jnp.float32), 0.099609375, 1.8984375).astype(jnp.bfloat16),
        "in_x": gaussian(streams_of[2], (D, INNER), D ** -0.5, 0.125, ((0, 64), (1, 4))),
        "in_z": gaussian(streams_of[3], (D, INNER), D ** -0.5, 0.125, ((0, 64), (1, 4))),
        "conv_weight": gaussian(streams_of[4], (CONV, INNER), CONV ** -0.5, 3.0, ((1, 4),), jnp.float32),
        "conv_bias": gaussian(streams_of[5], (INNER,), 0.5, 3.0, ((0, 4),), jnp.float32),
        "x_proj": gaussian(streams_of[6], (INNER, RANK + 2 * STATE), INNER ** -0.5, 0.09375, ((0, 256),)),
        "dt_proj": gaussian(streams_of[7], (RANK, INNER), RANK ** -0.5, 0.5, ((0, 64), (1, 4))),
        "dt_bias": jnp.clip(-5.0 + 4.0 * jax.random.uniform(streams_of[8], (INNER,), jnp.float32) ** block_levels(streams_of[8], (INNER,), ((0, 4),), -0.2, 0.2), -5.0, -1.0),
        "a_log": jnp.clip(2.77 * jax.random.uniform(streams_of[9], (STATE, INNER), jnp.float32) ** block_levels(streams_of[9], (STATE, INNER), ((1, 4),), -0.2, 0.2), 0.0, 2.77),
        "skip": jnp.clip(0.5 + 1.0 * jax.random.uniform(streams_of[10], (INNER,), jnp.float32) ** block_levels(streams_of[10], (INNER,), ((0, 4),), -0.2, 0.2), 0.5, 1.5),
        "out_proj": gaussian(streams_of[11], (INNER, D), INNER ** -0.5, 0.09375, ((0, 4), (1, 64))),
        "state_pool": gaussian(streams_of[12], (SLOTS, STATE, INNER), 1.0, 6.0, ((0, 64), (2, 4)), jnp.float32),
        "conv_pool": gaussian(streams_of[13], (SLOTS, CONV - 1, INNER), 1.0, 6.0, ((0, 64), (2, 4)), jnp.float32),
        "permutation": draw_permutation(jax.random.fold_in(streams_of[17], 71), 0),
        "page_table": draw_page_table(jax.random.fold_in(streams_of[17], 71), 0),
        "accepted": place_ends(jax.random.randint(streams_of[16], (REQUESTS,), 1, DRAFTS + 1), jax.random.fold_in(streams_of[16], 1), 1, DRAFTS).astype(jnp.int32),
    }


EPS = 1e-05

def layer_block(hidden, caches, accepted, norm_gain, in_x, in_z, conv_weight, conv_bias, x_proj, dt_proj, dt_bias, a_log, skip, out_proj):
    count = hidden.shape[0]
    tokens = count * DRAFTS
    rows = hidden.reshape(tokens, D).astype(jnp.float32)
    scale = lax.rsqrt(lax.optimization_barrier(jnp.mean(rows * rows, axis=1, keepdims=True)) + EPS)
    normed = (rows * scale * norm_gain.astype(jnp.float32)).astype(jnp.bfloat16)
    x_part = jnp.dot(normed, in_x, preferred_element_type=jnp.float32).astype(jnp.bfloat16)
    z_part = jnp.dot(normed, in_z, preferred_element_type=jnp.float32).astype(jnp.bfloat16)
    states = caches[:, :STATE, :]
    edges = caches[:, STATE:, :]
    padded = jnp.concatenate([edges, x_part.astype(jnp.float32).reshape(count, DRAFTS, INNER)], axis=1)
    mixed = conv_bias + jnp.zeros((count, DRAFTS, INNER), jnp.float32)
    for offset in range(CONV):
        mixed = mixed + conv_weight[offset] * padded[:, offset:offset + DRAFTS, :]
    inputs = jax.nn.silu(mixed).astype(jnp.bfloat16)
    flat_inputs = inputs.reshape(tokens, INNER)
    low = jnp.dot(flat_inputs, x_proj[:, :RANK], preferred_element_type=jnp.float32).astype(jnp.bfloat16)
    both = jnp.einsum('ks,tk->st', x_proj[:, RANK:].astype(jnp.float32), flat_inputs.astype(jnp.float32))
    delta = jax.nn.softplus(jnp.dot(low, dt_proj, preferred_element_type=jnp.float32) + dt_bias)
    delta = delta.reshape(count, DRAFTS, INNER)
    decay_rate = -jnp.exp(a_log)
    inputs_wide = inputs.astype(jnp.float32)
    driven = delta * inputs_wide
    b_time = both[:STATE].reshape(STATE, count, DRAFTS).transpose(2, 1, 0)
    c_time = both[STATE:].reshape(STATE, count, DRAFTS).transpose(2, 1, 0)

    def advance(carry, slices):
        state, kept = carry
        step_delta, step_drive, step_b, step_c, index = slices
        state = jnp.exp(step_delta[:, None, :] * decay_rate[None]) * state + step_drive[:, None, :] * step_b[:, :, None]
        output = lax.optimization_barrier(jnp.sum(state * step_c[:, :, None], axis=1))
        kept = jnp.where((accepted - 1 == index)[:, None, None], state, kept)
        return ((state, kept), output)
    (final_state, kept), outputs = lax.scan(advance, (states, states), (delta.transpose(1, 0, 2), driven.transpose(1, 0, 2), b_time, c_time, jnp.arange(DRAFTS, dtype=jnp.int32)))
    outputs = outputs.transpose(1, 0, 2)
    z_wide = z_part.astype(jnp.float32).reshape(count, DRAFTS, INNER)
    gated = ((outputs + skip * inputs_wide) * jax.nn.silu(z_wide)).astype(jnp.bfloat16).reshape(tokens, INNER)
    index = accepted[:, None].astype(jnp.int32) + jnp.arange(CONV - 1, dtype=jnp.int32)[None, :]
    new_edges = jnp.take_along_axis(padded, index[:, :, None], axis=1)
    new_caches = jnp.concatenate([kept, new_edges], axis=1)
    result = (jnp.dot(gated, out_proj, preferred_element_type=jnp.float32) + rows).astype(jnp.bfloat16)
    return (result.reshape(count, DRAFTS, D), new_caches)

def reference(hidden, norm_gain, in_x, in_z, conv_weight, conv_bias, x_proj, dt_proj, dt_bias, a_log, skip, out_proj, state_pool, conv_pool, permutation, page_table, accepted):
    caches = jnp.concatenate([state_pool[page_table], conv_pool[page_table]], axis=1)

    def run(block):
        block_hidden, block_caches, block_accept = block
        return layer_block(block_hidden, block_caches, block_accept, norm_gain, in_x, in_z, conv_weight, conv_bias, x_proj, dt_proj, dt_bias, a_log, skip, out_proj)
    home_rows, new_caches = lax.map(run, (hidden.reshape(N_DP, REQ_DEV, DRAFTS, D), caches.reshape(N_DP, REQ_DEV, STATE + CONV - 1, INNER), accepted.reshape(N_DP, REQ_DEV)))
    home_rows = home_rows.reshape(REQUESTS, DRAFTS, D)
    new_caches = new_caches.reshape(REQUESTS, STATE + CONV - 1, INNER)
    verified = jnp.zeros_like(hidden).at[permutation].set(home_rows)
    new_state_pool = state_pool.at[page_table].set(new_caches[:, :STATE])
    new_conv_pool = conv_pool.at[page_table].set(new_caches[:, STATE:])
    return (verified, new_state_pool, new_conv_pool)
```

```python
import jax
import jax.numpy as jnp
from jax import lax
from jax.experimental import pallas as pl
from jax.experimental.pallas import tpu as pltpu
from jax.sharding import PartitionSpec as P

EPS = 1e-05
LOG2E = 1.4426950408889634
BF = jnp.bfloat16
F32 = jnp.float32
SIDE = 4
CUT = 384

VMEM = pl.BlockSpec(memory_space=pltpu.VMEM)
SMEM = pl.BlockSpec(memory_space=pltpu.SMEM)
ANY = pl.BlockSpec(memory_space=pl.ANY)


def shift_pairs(axis, step):
    pairs = []
    for z in range(SIDE):
        for y in range(SIDE):
            for x in range(SIDE):
                to = [z, y, x]
                to[axis] = (to[axis] + step) % SIDE
                pairs.append(((z * SIDE + y) * SIDE + x, (to[0] * SIDE + to[1]) * SIDE + to[2]))
    return pairs


def hop(value, axis, step):
    return lax.ppermute(value, "dp", shift_pairs(axis, step))


def across(value, flip):
    return lax.ppermute(value, "mp", [(m, m ^ flip) for m in range(4)])


def ring(block, axis):
    half = block.shape[0] // 2
    after = hop(block, axis, -1)
    before = hop(block, axis, 1)
    low = hop(before[:half], axis, 1)
    high = hop(after[half:], axis, -1)
    return block, after, low, high, before


def gather_z(block):
    return jnp.stack([block, hop(block, 0, -1), hop(block, 0, 2), hop(block, 0, 1)])


def gather_plane(stack, middle, last):
    own, after, low, high, before = ring(stack, middle)
    whole = jnp.stack([own, after, jnp.concatenate([low, high]), before])
    return ring(whole, last)


def start_pieces(pieces, place, middle_first, body):
    z, y, x = place
    own, after, low, high, before = pieces

    def one(k, _):
        for i in range(SIDE):
            for f in range(SIDE):
                if f == 2:
                    ref, at = (low, i) if i < 2 else (high, i - 2)
                else:
                    ref, at = {0: own, 1: after, 3: before}[f], i
                dz = (z + k) & 3
                if middle_first:
                    dx, dy = (x + i) & 3, (y + f) & 3
                else:
                    dy, dx = (y + i) & 3, (x + f) & 3
                body(ref.at[at, k], (dz * SIDE + dy) * SIDE + dx)
        return 0

    lax.fori_loop(0, SIDE, one, 0)


def place_of(where):
    d = where[0]
    return d >> 4, (d >> 2) & 3, d & 3


def sigmoid_times(value):
    return value / (1.0 + jnp.exp(-value))


def order_matrix(rows, columns, drafts, count):
    i = lax.broadcasted_iota(jnp.int32, (rows, columns), 0)
    j = lax.broadcasted_iota(jnp.int32, (rows, columns), 1)
    return ((i % count) * drafts + i // count == j).astype(BF)


def front_kernel(
    where, pages, accepted, h0, h1, h2, h3, a0, a1, a2, a3, a4, b0, b1, b2, b3, b4,
    taps, bias, pool, normed_out, inputs_out, sums_out, dt_out, pool_out,
    weight, proj, dt_raw, dt_wide, xs, edges, fresh, plain, sems,
):
    place = place_of(where)
    m = where[1]
    drafts, count, width = xs.shape
    tokens = drafts * count
    slots = pool.shape[1]

    def take_a(src, d):
        pltpu.make_async_copy(src.at[pl.ds(0, 32), :], weight.at[pl.ds(d * 32, 32), pl.ds(0, CUT)], sems.at[0]).start()
        pltpu.make_async_copy(src.at[pl.ds(32, 16), pl.ds(0, 256)], proj.at[pl.ds(d * 16, 16), :], sems.at[1]).start()
        pltpu.make_async_copy(src.at[pl.ds(32, 16), pl.ds(256, 128)], dt_raw.at[pl.ds(d * 16, 16), :], sems.at[2]).start()

    def take_b(src, d):
        pltpu.make_async_copy(src, weight.at[pl.ds(d * 32, 32), pl.ds(CUT, width - CUT)], sems.at[0]).start()

    start_pieces((a0, a1, a2, a3, a4), place, True, take_a)
    start_pieces((b0, b1, b2, b3, b4), place, False, take_b)

    blocks = (h0, h1, h2, h3)
    step = 32

    def norm(n, _):
        at = pl.ds(pl.multiple_of(n * step, step), step)
        rows = [h[at, :].astype(F32) for h in blocks]
        total = sum(jnp.sum(r * r, axis=1, keepdims=True) for r in rows)
        scale = lax.rsqrt(total / 2048.0 + EPS)
        for k, h in enumerate(blocks):
            gain = h[pl.ds(tokens, 1), :].astype(F32)
            plain[k, at, :] = (rows[k] * scale * gain).astype(BF)
        return 0

    lax.fori_loop(0, tokens // step, norm, 0)
    order = order_matrix(tokens, tokens, drafts, count)
    for k in range(4):
        normed_out[k] = jnp.dot(order, plain[k], preferred_element_type=F32).astype(BF)

    def edge(r, _):
        slot = lax.rem(pages[r], slots)
        for k in range(3):
            edges[k, pl.ds(r, 1), :] = pool[k, pl.ds(slot, 1), :]
        return 0

    lax.fori_loop(0, count, edge, 0)
    pltpu.make_async_copy(weight, weight, sems.at[0]).wait()
    pltpu.make_async_copy(proj, proj, sems.at[1]).wait()
    pltpu.make_async_copy(dt_raw, dt_raw, sems.at[2]).wait()

    def project(n, _):
        at = pl.ds(pl.multiple_of(n * 256, 256), 256)
        total = jnp.zeros((tokens, 256), F32)
        for k in range(4):
            total = total + jnp.dot(
                normed_out[k], weight[pl.ds((m ^ k) * 512, 512), at], preferred_element_type=F32
            )
        xs[:, :, at] = total.astype(BF).astype(F32).reshape(drafts, count, 256)
        return 0

    lax.fori_loop(0, width // 256, project, 0)

    def mix(n, _):
        rows = pl.ds(pl.multiple_of((n // 4) * 16, 16), 16)
        at = pl.ds(pl.multiple_of((n % 4) * 256, 256), 256)
        acc = jnp.concatenate([accepted[rows, :]] * 2, axis=1)
        window = [edges[k, rows, at] for k in range(3)]
        kept = [window[0], window[0], window[0]]
        for p in range(1, 3):
            for k in range(3):
                kept[k] = jnp.where(acc + k == p, window[p], kept[k])
        tap = [taps[k : k + 1, at] for k in range(4)]
        base = bias[:, at]
        for t in range(drafts):
            now = xs[t, rows, at]
            mixed = base + tap[0] * window[0]
            mixed = mixed + tap[1] * window[1]
            mixed = mixed + tap[2] * window[2]
            mixed = mixed + tap[3] * now
            inputs_out[pl.ds(t * count + (n // 4) * 16, 16), at] = sigmoid_times(mixed).astype(BF)
            for k in range(3):
                kept[k] = jnp.where(acc + k == t + 3, now, kept[k])
            window = [window[1], window[2], now]
        for k in range(3):
            fresh[k, rows, at] = kept[k]
        return 0

    lax.fori_loop(0, (count // 16) * (width // 256), mix, 0)
    sums = lax.dot_general(
        proj[...], inputs_out[...], (((0,), (1,)), ((), ())), preferred_element_type=F32
    )
    sums_out[...] = sums[: sums_out.shape[0]]
    dt_wide[...] = dt_raw[...].astype(F32)
    for c in range(width // 128):
        dt_out[:, c * 128 : (c + 1) * 128] = dt_wide[pl.ds(c, 128, stride=8), :].astype(BF)
    pool_out[...] = pool[...]

    def settle(r, _):
        slot = lax.rem(pages[r], slots)
        for k in range(3):
            pool_out[k, pl.ds(slot, 1), :] = fresh[k, pl.ds(r, 1), :]
        return 0

    lax.fori_loop(0, count, settle, 0)


def scan_kernel(
    pages, accepted, sums_a, sums_b, dt, dt_bias, a_log, inputs, pool, ys_out, pool_out,
    low, both, delta, decay, start, wide, kept,
):
    tokens, width = inputs.shape
    count = accepted.shape[0]
    drafts = tokens // count
    states = a_log.shape[0]
    rank = low.shape[1]
    slots = pool.shape[0] // states

    def fetch(r, _):
        slot = lax.rem(pages[r], slots)
        for c in range(width // 128):
            start[c, pl.ds(pl.multiple_of(r * states, states), states), :] = pool[
                pl.ds(pl.multiple_of(slot * states, states), states), c * 128 : (c + 1) * 128
            ]
        return 0

    lax.fori_loop(0, count, fetch, 0)

    def carry_over(n, _):
        at = pl.ds(pl.multiple_of(n * states, states), states)
        pool_out[at, :] = pool[at, :]
        return 0

    lax.fori_loop(0, slots, carry_over, 0)
    summed = sums_a[...] + sums_b[...]
    low[...] = summed[:rank].T.astype(BF)
    rest = jnp.concatenate([summed[rank:], jnp.zeros((128 - 2 * states, tokens), F32)], axis=0)
    both[...] = rest.T

    def steps(n, _):
        at = pl.ds(pl.multiple_of(n * 256, 256), 256)
        value = jnp.dot(low[...], dt[:, at], preferred_element_type=F32) + dt_bias[:, at]
        delta[:, at] = jnp.maximum(value, 0.0) + jnp.log1p(jnp.exp(-jnp.abs(value)))
        return 0

    lax.fori_loop(0, width // 256, steps, 0)
    for s in range(states):
        row = -jnp.exp(a_log[s : s + 1, :]) * LOG2E
        decay[s] = jnp.broadcast_to(row, (8, width))

    def some(rb, _):
        def spread(t, _):
            tile = both[pl.ds(pl.multiple_of(t * count + rb * 8, 8), 8), :]
            for q in range(2 * states):
                wide[t, q] = jnp.broadcast_to(tile[:, q : q + 1], (8, 128))
            return 0

        lax.fori_loop(0, drafts, spread, 0)
        last = accepted[pl.ds(pl.multiple_of(rb * 8, 8), 8), :] - 1

        def columns(cb, _):
            at = pl.ds(pl.multiple_of(cb * 128, 128), 128)
            first = tuple(
                start[cb, pl.ds(rb * 8 * states + s, 8, stride=states), :] for s in range(states)
            )

            def advance(t, state):
                rows = pl.ds(pl.multiple_of(t * count + rb * 8, 8), 8)
                d = delta[rows, at]
                drive = d * wide_inputs(rows, at)
                here = last == t
                out = None
                nexts = []
                for s in range(states):
                    new = jnp.exp2(d * decay[s, :, at]) * state[s] + drive * wide[t, s]
                    term = new * wide[t, states + s]
                    out = term if out is None else out + term
                    pltpu.store(kept.at[cb, pl.ds(pl.multiple_of(s * count + rb * 8, 8), 8), :], new, mask=here)
                    nexts.append(new)
                ys_out[rows, at] = out
                return tuple(nexts)

            lax.fori_loop(0, drafts, advance, first, unroll=2)
            return 0

        lax.fori_loop(0, width // 128, columns, 0)
        return 0

    def wide_inputs(rows, at):
        return inputs[rows, at].astype(F32)

    lax.fori_loop(0, count // 8, some, 0)

    def settle(r, _):
        slot = lax.rem(pages[r], slots)
        for c in range(width // 128):
            for s in range(0, states, 8):
                pool_out[
                    pl.ds(pl.multiple_of(slot * states + s, 8), 8), c * 128 : (c + 1) * 128
                ] = kept[c, pl.ds(s * count + r, 8, stride=count), :]
        return 0

    lax.fori_loop(0, count, settle, 0)


def back_kernel(
    where, normed, inputs, ys, skip, a0, a1, a2, a3, a4, b0, b1, b2, b3, b4,
    send_out, keep_out, weight, outer, gated, sems,
):
    place = place_of(where)
    m = where[1]
    tokens, width = gated.shape
    half = width // 2

    def take(src, d, column):
        at = pl.ds(column, half)
        pltpu.make_async_copy(src.at[pl.ds(0, 32), :], weight.at[pl.ds(d * 32, 32), at], sems.at[0]).start()
        pltpu.make_async_copy(src.at[pl.ds(32, 32), :], outer.at[pl.ds(d * 32, 32), at], sems.at[1]).start()

    start_pieces((a0, a1, a2, a3, a4), place, True, lambda src, d: take(src, d, 0))
    start_pieces((b0, b1, b2, b3, b4), place, False, lambda src, d: take(src, d, half))
    pltpu.make_async_copy(weight, weight, sems.at[0]).wait()
    pltpu.make_async_copy(outer, outer, sems.at[1]).wait()

    def gate(n, _):
        at = pl.ds(pl.multiple_of(n * 256, 256), 256)
        total = jnp.zeros((tokens, 256), F32)
        for k in range(4):
            total = total + jnp.dot(
                normed[k], weight[pl.ds((m ^ k) * 512, 512), at], preferred_element_type=F32
            )
        z = total.astype(BF).astype(F32)
        mixed = ys[:, at] + skip[:, at] * inputs[:, at].astype(F32)
        gated[:, at] = (mixed * sigmoid_times(z)).astype(BF)
        return 0

    lax.fori_loop(0, width // 256, gate, 0)

    def out(n, _):
        far, part = n // 2, (n % 2) * 256
        column = pl.ds(pl.multiple_of(part, 256), 256)
        for core in range(2):
            rows = pl.ds(pl.multiple_of((m ^ (far * 2 + core)) * 512 + part, 256), 256)
            value = lax.dot_general(
                gated[...], outer[rows, :], (((1,), (1,)), ((), ())), preferred_element_type=F32
            )
            if core:
                send_out[far, :, column] = value.astype(BF)
            else:
                keep_out[far, :, column] = value
        return 0

    lax.fori_loop(0, 4, out, 0)


def join_kernel(targets, keep, near, far, hidden, out, total):
    tokens, width = hidden.shape
    count = targets.shape[0]
    drafts = tokens // count
    order = order_matrix(tokens, tokens, drafts, count)
    base = jnp.dot(order, hidden[...], preferred_element_type=F32)
    summed = keep[...] + near[...].astype(F32) + far[...].astype(F32)
    rounded = (summed + base).astype(BF)
    back = lax.dot_general(order, rounded, (((0,), (0,)), ((), ())), preferred_element_type=F32)
    total[...] = back.astype(BF).reshape(count, drafts, width)
    out[...] = jnp.zeros(out.shape, BF)

    def place(r, _):
        out[lax.div(targets[r], count)] = total[r]
        return 0

    lax.fori_loop(0, count, place, 0)


def unpack_kernel(where, targets, got, out, sem):
    count = targets.shape[0]
    peers = got.shape[0]

    def begin(r, _):
        source = lax.rem(2 * where[0] - lax.div(targets[r], count) + 2 * peers, peers)
        pltpu.make_async_copy(got.at[source], out.at[r], sem).start()
        return 0

    lax.fori_loop(0, count, begin, 0)
    pltpu.make_async_copy(out, out, sem).wait()


def params():
    return pltpu.CompilerParams(vmem_limit_bytes=56 << 20)


def on_device(
    hidden, norm_gain, in_x, in_z, conv_weight, conv_bias, x_proj, dt_proj, dt_bias, a_log, skip,
    out_proj, state_pool, conv_pool, permutation, page_table, accepted,
):
    count, drafts, part = hidden.shape
    tokens = count * drafts
    width = in_x.shape[1]
    slots, states, _ = state_pool.shape
    rank = x_proj.shape[1] - 2 * states
    where = jnp.stack([lax.axis_index("dp"), lax.axis_index("mp")]).astype(jnp.int32)
    peers = lax.axis_size("dp")

    extra = jnp.concatenate(
        [x_proj, jnp.zeros((16, 256 - x_proj.shape[1]), BF), dt_proj.reshape(16, 128)], axis=1
    )
    block_a = jnp.concatenate([in_x[:, :CUT], extra], axis=0)
    first_a = gather_plane(gather_z(block_a), 2, 1)
    first_b = gather_plane(gather_z(in_x[:, CUT:]), 1, 2)

    flat = hidden.reshape(tokens, part)
    sent = jnp.concatenate([flat, jnp.broadcast_to(norm_gain[None], (16, part))], axis=0)
    near = across(sent, 1)
    far = across(sent, 2)
    both = across(far, 1)

    pair = jnp.concatenate([in_z, out_proj.T], axis=0)
    stacked = gather_z(pair)
    second_a = gather_plane(stacked[..., : width // 2], 2, 1)
    second_b = gather_plane(stacked[..., width // 2 :], 1, 2)

    wide_accepted = jnp.broadcast_to(accepted[:, None], (count, 128))
    normed, inputs, sums, dt, new_conv = pl.pallas_call(
        front_kernel,
        out_shape=(
            jax.ShapeDtypeStruct((4, tokens, part), BF),
            jax.ShapeDtypeStruct((tokens, width), BF),
            jax.ShapeDtypeStruct((rank + 2 * states, tokens), F32),
            jax.ShapeDtypeStruct((rank, width), BF),
            jax.ShapeDtypeStruct((3, slots, width), F32),
        ),
        in_specs=[SMEM, SMEM] + [VMEM] * 5 + [ANY] * 10 + [VMEM] * 3,
        out_specs=(VMEM,) * 5,
        scratch_shapes=[
            pltpu.VMEM((2048, width), BF),
            pltpu.VMEM((1024, 256), BF),
            pltpu.VMEM((1024, 128), BF),
            pltpu.VMEM((1024, 128), F32),
            pltpu.VMEM((drafts, count, width), F32),
            pltpu.VMEM((3, count, width), F32),
            pltpu.VMEM((3, count, width), F32),
            pltpu.VMEM((4, tokens, part), BF),
            pltpu.SemaphoreType.DMA((3,)),
        ],
        compiler_params=params(),
        cost_estimate=pl.CostEstimate(flops=6_000_000_000, bytes_accessed=10 << 20, transcendentals=0),
        name="front",
    )(
        where, page_table, wide_accepted, sent, near, far, both, *reorder(first_a), *reorder(first_b),
        conv_weight, conv_bias[None], conv_pool.transpose(1, 0, 2),
    )

    sums = sums + across(sums, 1)
    other = across(sums, 2)
    ys, new_state = pl.pallas_call(
        scan_kernel,
        out_shape=(
            jax.ShapeDtypeStruct((tokens, width), F32),
            jax.ShapeDtypeStruct((slots * states, width), F32),
        ),
        in_specs=[SMEM] + [VMEM] * 8,
        out_specs=(VMEM,) * 2,
        scratch_shapes=[
            pltpu.VMEM((tokens, rank), BF),
            pltpu.VMEM((tokens, 128), F32),
            pltpu.VMEM((tokens, width), F32),
            pltpu.VMEM((states, 8, width), F32),
            pltpu.VMEM((width // 128, count * states, 128), F32),
            pltpu.VMEM((drafts, 2 * states, 8, 128), F32),
            pltpu.VMEM((width // 128, states * count, 128), F32),
        ],
        compiler_params=params(),
        cost_estimate=pl.CostEstimate(flops=12_000_000_000, bytes_accessed=10 << 20, transcendentals=0),
        name="scan",
    )(
        page_table, wide_accepted, sums, other, dt, dt_bias[None], a_log, inputs,
        state_pool.reshape(slots * states, width),
    )

    send, keep = pl.pallas_call(
        back_kernel,
        out_shape=(
            jax.ShapeDtypeStruct((2, tokens, part), BF),
            jax.ShapeDtypeStruct((2, tokens, part), F32),
        ),
        in_specs=[SMEM] + [VMEM] * 4 + [ANY] * 10,
        out_specs=(VMEM,) * 2,
        scratch_shapes=[
            pltpu.VMEM((2048, width), BF),
            pltpu.VMEM((2048, width), BF),
            pltpu.VMEM((tokens, width), BF),
            pltpu.SemaphoreType.DMA((2,)),
        ],
        compiler_params=params(),
        cost_estimate=pl.CostEstimate(flops=6_000_000_000, bytes_accessed=16 << 20, transcendentals=0),
        name="back",
    )(where, normed, inputs, ys, skip[None], *reorder(second_a), *reorder(second_b))

    got = across(send, 1)
    forward = (keep[1] + got[1].astype(F32)).astype(BF)
    remote = across(forward, 2)
    packed = pl.pallas_call(
        join_kernel,
        out_shape=jax.ShapeDtypeStruct((peers, drafts, part), BF),
        in_specs=[SMEM] + [VMEM] * 4,
        out_specs=VMEM,
        scratch_shapes=[pltpu.VMEM((count, drafts, part), BF)],
        compiler_params=params(),
        cost_estimate=pl.CostEstimate(flops=600_000_000, bytes_accessed=4 << 20, transcendentals=0),
        name="join",
    )(permutation, keep[0], got[0], remote, flat)
    arrived = lax.all_to_all(packed, "dp", split_axis=0, concat_axis=0, tiled=True)
    verified = pl.pallas_call(
        unpack_kernel,
        out_shape=jax.ShapeDtypeStruct((count, drafts, part), BF),
        in_specs=[SMEM, SMEM, ANY],
        out_specs=ANY,
        scratch_shapes=[pltpu.SemaphoreType.DMA(())],
        name="unpack",
    )(where, permutation, arrived)
    return (
        verified,
        new_state.reshape(slots, states, width),
        new_conv.transpose(1, 0, 2),
    )


def reorder(pieces):
    own, after, low, high, before = pieces
    return own, after, low, high, before


def solution(mesh):
    return jax.shard_map(
        on_device,
        mesh=mesh,
        in_specs=(
            P("dp", None, "mp"),
            P("mp"),
            P("dp", "mp"),
            P("dp", "mp"),
            P(None, "mp"),
            P("mp"),
            P(("mp", "dp"), None),
            P("dp", "mp"),
            P("mp"),
            P(None, "mp"),
            P("mp"),
            P("mp", "dp"),
            P("dp", None, "mp"),
            P("dp", None, "mp"),
            P("dp"),
            P("dp"),
            P("dp"),
        ),
        out_specs=(P("dp", None, "mp"), P("dp", None, "mp"), P("dp", None, "mp")),
        check_vma=False,
    )
```

```python
import jax
import jax.numpy as jnp
from jax import lax
from jax.experimental import pallas as pl
from jax.experimental.pallas import tpu as pltpu
from jax.sharding import PartitionSpec as P

EPS = 1e-05
LOG2E = 1.4426950408889634
BF = jnp.bfloat16
F32 = jnp.float32
SIDE = 4
CUT = 384

VMEM = pl.BlockSpec(memory_space=pltpu.VMEM)
SMEM = pl.BlockSpec(memory_space=pltpu.SMEM)
ANY = pl.BlockSpec(memory_space=pl.ANY)


def shift_pairs(axis, step):
    pairs = []
    for z in range(SIDE):
        for y in range(SIDE):
            for x in range(SIDE):
                to = [z, y, x]
                to[axis] = (to[axis] + step) % SIDE
                pairs.append(((z * SIDE + y) * SIDE + x, (to[0] * SIDE + to[1]) * SIDE + to[2]))
    return pairs


def hop(value, axis, step):
    return lax.ppermute(value, "dp", shift_pairs(axis, step))


def across(value, flip):
    return lax.ppermute(value, "mp", [(m, m ^ flip) for m in range(4)])


def ring(block, axis):
    half = block.shape[0] // 2
    after = hop(block, axis, -1)
    before = hop(block, axis, 1)
    low = hop(before[:half], axis, 1)
    high = hop(after[half:], axis, -1)
    return block, after, low, high, before


def direct(block, axis):
    return jnp.stack([block, hop(block, axis, -1), hop(block, axis, 2), hop(block, axis, 1)])


def start_pieces(pieces, place, middle_first, body):
    z, y, x = place
    own, after, low, high, before = pieces

    def one(k, _):
        for i in range(SIDE):
            for f in range(SIDE):
                if f == 2:
                    ref, at = (low, i) if i < 2 else (high, i - 2)
                else:
                    ref, at = {0: own, 1: after, 3: before}[f], i
                dz = (z + k) & 3
                if middle_first:
                    dx, dy = (x + i) & 3, (y + f) & 3
                else:
                    dy, dx = (y + i) & 3, (x + f) & 3
                body(ref.at[at, k], (dz * SIDE + dy) * SIDE + dx)
        return 0

    lax.fori_loop(0, SIDE, one, 0)


def place_of(where):
    d = where[0]
    return d >> 4, (d >> 2) & 3, d & 3


def sigmoid_times(value):
    return value / (1.0 + jnp.exp(-value))


def order_matrix(rows, columns, drafts, count):
    i = lax.broadcasted_iota(jnp.int32, (rows, columns), 0)
    j = lax.broadcasted_iota(jnp.int32, (rows, columns), 1)
    return ((i % count) * drafts + i // count == j).astype(BF)


def prep_kernel(h0, h1, h2, h3, normed_out, plain):
    tokens = normed_out.shape[1]
    count = 32
    blocks = (h0, h1, h2, h3)
    step = 32

    def norm(n, _):
        at = pl.ds(pl.multiple_of(n * step, step), step)
        rows = [h[at, :].astype(F32) for h in blocks]
        total = sum(jnp.sum(r * r, axis=1, keepdims=True) for r in rows)
        scale = lax.rsqrt(total / (4.0 * rows[0].shape[1]) + EPS)
        for k, h in enumerate(blocks):
            gain = h[pl.ds(tokens, 1), :].astype(F32)
            plain[k, at, :] = (rows[k] * scale * gain).astype(BF)
        return 0

    lax.fori_loop(0, tokens // step, norm, 0)
    order = order_matrix(tokens, tokens, tokens // count, count)
    for k in range(4):
        normed_out[k] = jnp.dot(order, plain[k], preferred_element_type=F32).astype(BF)


def front_kernel(
    where, pages, accepted, normed, a0, a1, a2, a3, a4, b0, b1, b2, b3, b4,
    taps, bias, pool, inputs_out, sums_out, dt_out, pool_out,
    weight, proj, dt_raw, dt_wide, xs, edges, fresh, sems,
):
    place = place_of(where)
    m = where[1]
    drafts, count, width = xs.shape
    tokens = drafts * count
    slots = pool.shape[1]

    def take_a(src, d):
        pltpu.make_async_copy(src.at[pl.ds(0, 32), :], weight.at[pl.ds(d * 32, 32), pl.ds(0, CUT)], sems.at[0]).start()
        pltpu.make_async_copy(src.at[pl.ds(32, 16), pl.ds(0, 256)], proj.at[pl.ds(d * 16, 16), :], sems.at[1]).start()
        pltpu.make_async_copy(src.at[pl.ds(32, 16), pl.ds(256, 128)], dt_raw.at[pl.ds(d * 16, 16), :], sems.at[2]).start()

    def take_b(src, d):
        pltpu.make_async_copy(src, weight.at[pl.ds(d * 32, 32), pl.ds(CUT, width - CUT)], sems.at[0]).start()

    start_pieces((a0, a1, a2, a3, a4), place, True, take_a)
    start_pieces((b0, b1, b2, b3, b4), place, False, take_b)

    def edge(r, _):
        slot = lax.rem(pages[r], slots)
        for k in range(3):
            edges[k, pl.ds(r, 1), :] = pool[k, pl.ds(slot, 1), :]
        return 0

    lax.fori_loop(0, count, edge, 0)
    pltpu.make_async_copy(weight, weight, sems.at[0]).wait()
    pltpu.make_async_copy(proj, proj, sems.at[1]).wait()
    pltpu.make_async_copy(dt_raw, dt_raw, sems.at[2]).wait()

    def project(n, _):
        at = pl.ds(pl.multiple_of(n * 256, 256), 256)
        total = jnp.zeros((tokens, 256), F32)
        for k in range(4):
            total = total + jnp.dot(
                normed[k], weight[pl.ds((m ^ k) * 512, 512), at], preferred_element_type=F32
            )
        xs[:, :, at] = total.astype(BF).astype(F32).reshape(drafts, count, 256)
        return 0

    lax.fori_loop(0, width // 256, project, 0)

    def mix(n, _):
        rows = pl.ds(pl.multiple_of((n // 4) * 16, 16), 16)
        at = pl.ds(pl.multiple_of((n % 4) * 256, 256), 256)
        acc = jnp.concatenate([accepted[rows, :]] * 2, axis=1)
        window = [edges[k, rows, at] for k in range(3)]
        kept = [window[0], window[0], window[0]]
        for p in range(1, 3):
            for k in range(3):
                kept[k] = jnp.where(acc + k == p, window[p], kept[k])
        tap = [taps[k : k + 1, at] for k in range(4)]
        base = bias[:, at]
        for t in range(drafts):
            now = xs[t, rows, at]
            mixed = base + tap[0] * window[0]
            mixed = mixed + tap[1] * window[1]
            mixed = mixed + tap[2] * window[2]
            mixed = mixed + tap[3] * now
            inputs_out[pl.ds(pl.multiple_of(t * count + (n // 4) * 16, 16), 16), at] = sigmoid_times(mixed).astype(BF)
            for k in range(3):
                kept[k] = jnp.where(acc + k == t + 3, now, kept[k])
            window = [window[1], window[2], now]
        for k in range(3):
            fresh[k, rows, at] = kept[k]
        return 0

    lax.fori_loop(0, (count // 16) * (width // 256), mix, 0)
    sums = lax.dot_general(
        proj[...], inputs_out[...], (((0,), (1,)), ((), ())), preferred_element_type=F32
    )
    sums_out[...] = sums[: sums_out.shape[0]]
    dt_wide[...] = dt_raw[...].astype(F32)
    for c in range(width // 128):
        dt_out[:, c * 128 : (c + 1) * 128] = dt_wide[pl.ds(c, 128, stride=8), :].astype(BF)
    pool_out[...] = pool[...]

    def settle(r, _):
        slot = lax.rem(pages[r], slots)
        for k in range(3):
            pool_out[k, pl.ds(slot, 1), :] = fresh[k, pl.ds(r, 1), :]
        return 0

    lax.fori_loop(0, count, settle, 0)


def scan_kernel(
    pages, accepted, sums_a, sums_b, dt, dt_bias, a_log, inputs, pool, ys_out, kept,
    low, both, delta, decay, start, wide, pick,
):
    tokens, width = inputs.shape
    count = accepted.shape[0]
    drafts = tokens // count
    states = a_log.shape[0]
    rank = low.shape[1]
    slots = pool.shape[0] // states

    def fetch(r, _):
        slot = lax.rem(pages[r], slots)
        for c in range(width // 128):
            start[c, pl.ds(pl.multiple_of(r * states, states), states), :] = pool[
                pl.ds(pl.multiple_of(slot * states, states), states), c * 128 : (c + 1) * 128
            ]
        return 0

    lax.fori_loop(0, count, fetch, 0)
    summed = sums_a[...] + sums_b[...]
    low[...] = summed[:rank].T.astype(BF)
    rest = summed[rank:]
    high = rest.astype(BF).astype(F32)
    middle = (rest - high).astype(BF).astype(F32)
    parts = [high, middle, rest - high - middle, jnp.zeros_like(rest)]
    both[...] = jnp.concatenate(parts, axis=0).T
    row = lax.broadcasted_iota(jnp.int32, (128, 128), 0)
    for q in range(2 * states):
        hit = ((row & (2 * states - 1)) == q) & (row < 6 * states)
        pick[:, q * 128 : (q + 1) * 128] = hit.astype(F32).astype(BF)

    def steps(n, _):
        at = pl.ds(pl.multiple_of(n * 256, 256), 256)
        value = jnp.dot(low[...], dt[:, at], preferred_element_type=F32) + dt_bias[:, at]
        delta[:, at] = jnp.maximum(value, 0.0) + jnp.log1p(jnp.exp(-jnp.abs(value)))
        return 0

    lax.fori_loop(0, width // 256, steps, 0)
    for s in range(states):
        decay[s] = jnp.broadcast_to(-jnp.exp(a_log[s : s + 1, :]) * LOG2E, (8, width))

    def some(rb, _):
        eight = pl.ds(pl.multiple_of(rb * 8, 8), 8)
        terms = jnp.concatenate(
            [both[pl.ds(pl.multiple_of(t * count + rb * 8, 8), 8), :] for t in range(drafts)], axis=0
        ).astype(BF)
        for q in range(0, 2 * states, 4):
            spread = jnp.dot(terms, pick[:, q * 128 : (q + 4) * 128], preferred_element_type=F32)
            for p in range(4):
                wide[:, q + p] = spread[:, p * 128 : (p + 1) * 128].reshape(drafts, 8, 128)
        last = accepted[eight, :] - 1

        def columns(cb, _):
            at = pl.ds(pl.multiple_of(cb * 128, 128), 128)
            first = tuple(
                start[cb, pl.ds(rb * 8 * states + s, 8, stride=states), :] for s in range(states)
            )

            def advance(t, state):
                rows = pl.ds(pl.multiple_of(t * count + rb * 8, 8), 8)
                d = delta[rows, at]
                drive = d * inputs[rows, at].astype(F32)
                here = last == t
                out = None
                nexts = []
                for s in range(states):
                    new = jnp.exp2(d * decay[s, :, at]) * state[s] + drive * wide[t, s]
                    term = new * wide[t, states + s]
                    out = term if out is None else out + term
                    pltpu.store(kept.at[cb, pl.ds(pl.multiple_of(s * count + rb * 8, 8), 8), :], new, mask=here)
                    nexts.append(new)
                ys_out[rows, at] = out
                return tuple(nexts)

            lax.fori_loop(0, drafts, advance, first, unroll=4)
            return 0

        lax.fori_loop(0, width // 128, columns, 0)
        return 0

    lax.fori_loop(0, count // 8, some, 0)


def settle_kernel(pages, kept, pool, pool_out):
    chunks, rows, _ = kept.shape
    count = pages.shape[0]
    states = rows // count
    slots = pool.shape[0] // states

    def carry_over(n, _):
        at = pl.ds(pl.multiple_of(n * states, states), states)
        pool_out[at, :] = pool[at, :]
        return 0

    lax.fori_loop(0, slots, carry_over, 0)

    def settle(r, _):
        slot = lax.rem(pages[r], slots)
        for c in range(chunks):
            for s in range(0, states, 8):
                pool_out[
                    pl.ds(pl.multiple_of(slot * states + s, 8), 8), c * 128 : (c + 1) * 128
                ] = kept[c, pl.ds(s * count + r, 8, stride=count), :]
        return 0

    lax.fori_loop(0, count, settle, 0)


def out_columns(where, gated, outer, far, put):
    z, m = where[0] >> 4, where[1]

    def out(part, _):
        column = pl.ds(pl.multiple_of(part * 256, 256), 256)
        for core in range(2):
            k = ((m ^ (far * 2 + core)) - z) & 3
            rows = outer[pl.ds(part * 8, 8), k, 32:64, :].reshape(256, gated.shape[1])
            put(core, column, lax.dot_general(
                gated[...], rows, (((1,), (1,)), ((), ())), preferred_element_type=F32
            ))
        return 0

    lax.fori_loop(0, 2, out, 0)


def gate_kernel(where, normed, inputs, ys, skip, second, gated, send_out, keep_out):
    z, m = where[0] >> 4, where[1]
    tokens, width = gated.shape

    def gate(n, _):
        at = pl.ds(pl.multiple_of(n * 256, 256), 256)
        total = jnp.zeros((tokens, 256), F32)
        for k in range(4):
            block = second[:, ((m ^ k) - z) & 3, 0:32, at].reshape(512, 256)
            total = total + jnp.dot(normed[k], block, preferred_element_type=F32)
        gates = total.astype(BF).astype(F32)
        mixed = ys[:, at] + skip[:, at] * inputs[:, at].astype(F32)
        gated[:, at] = (mixed * sigmoid_times(gates)).astype(BF)
        return 0

    lax.fori_loop(0, width // 256, gate, 0)

    def put(core, column, value):
        if core:
            send_out[:, column] = value.astype(BF)
        else:
            keep_out[:, column] = value

    out_columns(where, gated, second, 1, put)


def near_kernel(where, gated, second, send_out, keep_out):
    def put(core, column, value):
        if core:
            send_out[:, column] = value.astype(BF)
        else:
            keep_out[:, column] = value

    out_columns(where, gated, second, 0, put)


def join_kernel(targets, keep, near, far, hidden, out, total):
    tokens, width = hidden.shape
    count = targets.shape[0]
    drafts = tokens // count
    order = order_matrix(tokens, tokens, drafts, count)
    base = jnp.dot(order, hidden[...], preferred_element_type=F32)
    summed = keep[...] + near[...].astype(F32) + far[...].astype(F32)
    rounded = (summed + base).astype(BF)
    back = lax.dot_general(order, rounded, (((0,), (0,)), ((), ())), preferred_element_type=F32)
    total[...] = back.astype(BF).reshape(count, drafts, width)
    out[...] = jnp.zeros(out.shape, BF)

    def place(r, _):
        out[lax.div(targets[r], count)] = total[r]
        return 0

    lax.fori_loop(0, count, place, 0)


def unpack_kernel(where, targets, got, out):
    count = targets.shape[0]
    peers = got.shape[0]

    def take(r, _):
        source = lax.rem(2 * where[0] - lax.div(targets[r], count) + 2 * peers, peers)
        out[r] = got[source]
        return 0

    lax.fori_loop(0, count, take, 0)


def params():
    return pltpu.CompilerParams(vmem_limit_bytes=56 << 20)


def on_device(
    hidden, norm_gain, in_x, in_z, conv_weight, conv_bias, x_proj, dt_proj, dt_bias, a_log, skip,
    out_proj, state_pool, conv_pool, permutation, page_table, accepted,
):
    count, drafts, part = hidden.shape
    tokens = count * drafts
    width = in_x.shape[1]
    slots, states, _ = state_pool.shape
    rank = x_proj.shape[1] - 2 * states
    where = jnp.stack([lax.axis_index("dp"), lax.axis_index("mp")]).astype(jnp.int32)
    peers = lax.axis_size("dp")

    extra = jnp.concatenate(
        [
            x_proj,
            jnp.zeros((16, 256 - x_proj.shape[1]), BF),
            dt_proj.reshape(16, 128),
            jnp.zeros((16, width - CUT), BF),
        ],
        axis=1,
    )
    first = direct(jnp.concatenate([in_x, extra], axis=0), 0)
    first_a = ring(direct(first[:, :, :CUT], 2), 1)
    first_b = ring(direct(first[:, :32, CUT:], 1), 2)

    flat = hidden.reshape(tokens, part)
    sent = jnp.concatenate([flat, jnp.broadcast_to(norm_gain[None], (16, part))], axis=0)
    near = across(sent, 1)
    far = across(sent, 2)
    both = across(far, 1)
    normed = pl.pallas_call(
        prep_kernel,
        out_shape=jax.ShapeDtypeStruct((4, tokens, part), BF),
        in_specs=[VMEM] * 4,
        out_specs=VMEM,
        scratch_shapes=[pltpu.VMEM((4, tokens, part), BF)],
        compiler_params=params(),
        cost_estimate=pl.CostEstimate(flops=1_000_000_000, bytes_accessed=4 << 20, transcendentals=0),
        name="prep",
    )(sent, near, far, both)

    stacked = direct(jnp.concatenate([in_z, out_proj.T], axis=0), 0)
    second = lax.all_gather(
        stacked, "dp", axis=0,
        axis_index_groups=[[z * 16 + i for i in range(16)] for z in range(SIDE)],
    )

    wide_accepted = jnp.broadcast_to(accepted[:, None], (count, 128))
    inputs, sums, dt, new_conv = pl.pallas_call(
        front_kernel,
        out_shape=(
            jax.ShapeDtypeStruct((tokens, width), BF),
            jax.ShapeDtypeStruct((rank + 2 * states, tokens), F32),
            jax.ShapeDtypeStruct((rank, width), BF),
            jax.ShapeDtypeStruct((3, slots, width), F32),
        ),
        in_specs=[SMEM, SMEM] + [VMEM] * 2 + [ANY] * 10 + [VMEM] * 3,
        out_specs=(VMEM,) * 4,
        scratch_shapes=[
            pltpu.VMEM((2048, width), BF),
            pltpu.VMEM((1024, 256), BF),
            pltpu.VMEM((1024, 128), BF),
            pltpu.VMEM((1024, 128), F32),
            pltpu.VMEM((drafts, count, width), F32),
            pltpu.VMEM((3, count, width), F32),
            pltpu.VMEM((3, count, width), F32),
            pltpu.SemaphoreType.DMA((3,)),
        ],
        compiler_params=params(),
        cost_estimate=pl.CostEstimate(flops=6_000_000_000, bytes_accessed=10 << 20, transcendentals=0),
        name="front",
    )(
        where, page_table, wide_accepted, normed, *first_a, *first_b,
        conv_weight, conv_bias[None], conv_pool.transpose(1, 0, 2),
    )

    sums = sums + across(sums, 1)
    other = across(sums, 2)
    ys, kept = pl.pallas_call(
        scan_kernel,
        out_shape=(
            jax.ShapeDtypeStruct((tokens, width), F32),
            jax.ShapeDtypeStruct((width // 128, states * count, 128), F32),
        ),
        in_specs=[SMEM] + [VMEM] * 8,
        out_specs=(VMEM,) * 2,
        scratch_shapes=[
            pltpu.VMEM((tokens, rank), BF),
            pltpu.VMEM((tokens, 128), F32),
            pltpu.VMEM((tokens, width), F32),
            pltpu.VMEM((states, 8, width), F32),
            pltpu.VMEM((width // 128, count * states, 128), F32),
            pltpu.VMEM((drafts, 2 * states, 8, 128), F32),
            pltpu.VMEM((128, 2 * states * 128), BF),
        ],
        compiler_params=params(),
        cost_estimate=pl.CostEstimate(flops=12_000_000_000, bytes_accessed=10 << 20, transcendentals=0),
        name="scan",
    )(
        page_table, wide_accepted, sums, other, dt, dt_bias[None], a_log, inputs,
        state_pool.reshape(slots * states, width),
    )

    new_state = pl.pallas_call(
        settle_kernel,
        out_shape=jax.ShapeDtypeStruct((slots * states, width), F32),
        in_specs=[SMEM, VMEM, VMEM],
        out_specs=VMEM,
        compiler_params=params(),
        cost_estimate=pl.CostEstimate(flops=0, bytes_accessed=8 << 20, transcendentals=0),
        name="settle",
    )(page_table, kept, state_pool.reshape(slots * states, width))

    halves = (jax.ShapeDtypeStruct((tokens, part), BF), jax.ShapeDtypeStruct((tokens, part), F32))
    gated, send_far, keep_far = pl.pallas_call(
        gate_kernel,
        out_shape=(jax.ShapeDtypeStruct((tokens, width), BF), *halves),
        in_specs=[SMEM] + [VMEM] * 5,
        out_specs=(VMEM,) * 3,
        compiler_params=params(),
        cost_estimate=pl.CostEstimate(flops=4_000_000_000, bytes_accessed=16 << 20, transcendentals=0),
        name="gate",
    )(where, normed, inputs, ys, skip[None], second)
    forward = (keep_far + across(send_far, 1).astype(F32)).astype(BF)
    forward, gated = lax.optimization_barrier((forward, gated))
    remote = across(forward, 2)
    send_near, keep_near = pl.pallas_call(
        near_kernel,
        out_shape=halves,
        in_specs=[SMEM] + [VMEM] * 2,
        out_specs=(VMEM,) * 2,
        compiler_params=params(),
        cost_estimate=pl.CostEstimate(flops=2_000_000_000, bytes_accessed=10 << 20, transcendentals=0),
        name="near",
    )(where, gated, second)
    got = across(send_near, 1)
    packed = pl.pallas_call(
        join_kernel,
        out_shape=jax.ShapeDtypeStruct((peers, drafts, part), BF),
        in_specs=[SMEM] + [VMEM] * 4,
        out_specs=VMEM,
        scratch_shapes=[pltpu.VMEM((count, drafts, part), BF)],
        compiler_params=params(),
        cost_estimate=pl.CostEstimate(flops=600_000_000, bytes_accessed=4 << 20, transcendentals=0),
        name="join",
    )(permutation, keep_near, got, remote, flat)
    arrived = lax.all_to_all(packed, "dp", split_axis=0, concat_axis=0, tiled=True)
    verified = pl.pallas_call(
        unpack_kernel,
        out_shape=jax.ShapeDtypeStruct((count, drafts, part), BF),
        in_specs=[SMEM, SMEM, VMEM],
        out_specs=VMEM,
        name="unpack",
    )(where, permutation, arrived)
    return (
        verified,
        new_state.reshape(slots, states, width),
        new_conv.transpose(1, 0, 2),
    )


def solution(mesh):
    return jax.shard_map(
        on_device,
        mesh=mesh,
        in_specs=(
            P("dp", None, "mp"),
            P("mp"),
            P("dp", "mp"),
            P("dp", "mp"),
            P(None, "mp"),
            P("mp"),
            P(("mp", "dp"), None),
            P("dp", "mp"),
            P("mp"),
            P(None, "mp"),
            P("mp"),
            P("mp", "dp"),
            P("dp", None, "mp"),
            P("dp", None, "mp"),
            P("dp"),
            P("dp"),
            P("dp"),
        ),
        out_specs=(P("dp", None, "mp"), P("dp", None, "mp"), P("dp", None, "mp")),
        check_vma=False,
    )
```

```python
import jax
import jax.numpy as jnp
from jax import lax
from jax.experimental import pallas as pl
from jax.experimental.pallas import tpu as pltpu
from jax.sharding import PartitionSpec as P

EPS = 1e-05
LOG2E = 1.4426950408889634
BF = jnp.bfloat16
F32 = jnp.float32
SIDE = 4
CUT = 384

VMEM = pl.BlockSpec(memory_space=pltpu.VMEM)
SMEM = pl.BlockSpec(memory_space=pltpu.SMEM)
ANY = pl.BlockSpec(memory_space=pl.ANY)


def shift_pairs(axis, step):
    pairs = []
    for z in range(SIDE):
        for y in range(SIDE):
            for x in range(SIDE):
                to = [z, y, x]
                to[axis] = (to[axis] + step) % SIDE
                pairs.append(((z * SIDE + y) * SIDE + x, (to[0] * SIDE + to[1]) * SIDE + to[2]))
    return pairs


def hop(value, axis, step):
    return lax.ppermute(value, "dp", shift_pairs(axis, step))


def across(value, flip):
    return lax.ppermute(value, "mp", [(m, m ^ flip) for m in range(4)])


def after(value, *others):
    return lax.optimization_barrier((value, others))[0]


def ring_one(block, axis):
    return hop(block, axis, -1), hop(block, axis, 1)


def ring_two(block, axis, sides):
    half = block.shape[0] // 2
    above, below = sides
    return block, above, hop(below[:half], axis, 1), hop(above[half:], axis, -1), below


def direct(block, axis):
    return jnp.stack([block, hop(block, axis, -1), hop(block, axis, 2), hop(block, axis, 1)])


def start_pieces(pieces, place, middle_first, body):
    z, y, x = place
    own, above, low, high, below = pieces

    def one(k, _):
        dz = (z + k) & 3
        for i in range(SIDE):
            for f in range(SIDE):
                if f == 2:
                    ref, at = (low, i) if i < 2 else (high, i - 2)
                else:
                    ref, at = {0: own, 1: above, 3: below}[f], i
                if middle_first:
                    dx, dy = (x + i) & 3, (y + f) & 3
                else:
                    dy, dx = (y + i) & 3, (x + f) & 3
                body(ref.at[at, k], (dz * SIDE + dy) * SIDE + dx)
        return 0

    lax.fori_loop(0, SIDE, one, 0)


def place_of(where):
    d = where[0]
    return d >> 4, (d >> 2) & 3, d & 3


def sigmoid_times(value):
    return value / (1.0 + jnp.exp(-value))


def order_matrix(rows, columns, drafts, count):
    i = lax.broadcasted_iota(jnp.int32, (rows, columns), 0)
    j = lax.broadcasted_iota(jnp.int32, (rows, columns), 1)
    return ((i % count) * drafts + i // count == j).astype(BF)


def prep_kernel(h0, h1, h2, h3, normed_out, plain):
    tokens = normed_out.shape[1]
    count = 32
    blocks = (h0, h1, h2, h3)
    step = 32

    def norm(n, _):
        at = pl.ds(pl.multiple_of(n * step, step), step)
        rows = [h[at, :].astype(F32) for h in blocks]
        total = sum(jnp.sum(r * r, axis=1, keepdims=True) for r in rows)
        scale = lax.rsqrt(total / (4.0 * rows[0].shape[1]) + EPS)
        for k, h in enumerate(blocks):
            gain = h[pl.ds(tokens, 1), :].astype(F32)
            plain[k, at, :] = (rows[k] * scale * gain).astype(BF)
        return 0

    lax.fori_loop(0, tokens // step, norm, 0)
    order = order_matrix(tokens, tokens, tokens // count, count)
    for k in range(4):
        normed_out[k] = jnp.dot(order, plain[k], preferred_element_type=F32).astype(BF)


def front_kernel(
    where, pages, accepted, normed, a0, a1, a2, a3, a4, b0, b1, b2, b3, b4,
    taps, bias, pool, inputs_out, sums_out, dt_out, pool_out,
    weight, proj, dt_raw, dt_wide, xs, edges, fresh, sems,
):
    place = place_of(where)
    m = where[1]
    drafts, count, width = xs.shape
    tokens = drafts * count
    slots = pool.shape[1]

    def take_a(src, d):
        pltpu.make_async_copy(src.at[pl.ds(0, 32), :], weight.at[pl.ds(d * 32, 32), pl.ds(0, CUT)], sems.at[0]).start()
        pltpu.make_async_copy(src.at[pl.ds(32, 16), pl.ds(0, 256)], proj.at[pl.ds(d * 16, 16), :], sems.at[1]).start()
        pltpu.make_async_copy(src.at[pl.ds(32, 16), pl.ds(256, 128)], dt_raw.at[pl.ds(d * 16, 16), :], sems.at[2]).start()

    def take_b(src, d):
        pltpu.make_async_copy(src, weight.at[pl.ds(d * 32, 32), pl.ds(CUT, width - CUT)], sems.at[0]).start()

    start_pieces((a0, a1, a2, a3, a4), place, True, take_a)
    start_pieces((b0, b1, b2, b3, b4), place, False, take_b)

    def edge(r, _):
        slot = lax.rem(pages[r], slots)
        for k in range(3):
            edges[k, pl.ds(r, 1), :] = pool[k, pl.ds(slot, 1), :]
        return 0

    lax.fori_loop(0, count, edge, 0)
    pltpu.make_async_copy(weight, weight, sems.at[0]).wait()
    pltpu.make_async_copy(proj, proj, sems.at[1]).wait()
    pltpu.make_async_copy(dt_raw, dt_raw, sems.at[2]).wait()

    def project(n, _):
        at = pl.ds(pl.multiple_of(n * 256, 256), 256)
        total = jnp.zeros((tokens, 256), F32)
        for k in range(4):
            total = total + jnp.dot(
                normed[k], weight[pl.ds((m ^ k) * 512, 512), at], preferred_element_type=F32
            )
        xs[:, :, at] = total.astype(BF).astype(F32).reshape(drafts, count, 256)
        return 0

    lax.fori_loop(0, width // 256, project, 0)

    def mix(n, _):
        rows = pl.ds(pl.multiple_of((n // 4) * 16, 16), 16)
        at = pl.ds(pl.multiple_of((n % 4) * 256, 256), 256)
        acc = jnp.concatenate([accepted[rows, :]] * 2, axis=1)
        window = [edges[k, rows, at] for k in range(3)]
        kept = [window[0], window[0], window[0]]
        for p in range(1, 3):
            for k in range(3):
                kept[k] = jnp.where(acc + k == p, window[p], kept[k])
        tap = [taps[k : k + 1, at] for k in range(4)]
        base = bias[:, at]
        for t in range(drafts):
            now = xs[t, rows, at]
            mixed = base + tap[0] * window[0]
            mixed = mixed + tap[1] * window[1]
            mixed = mixed + tap[2] * window[2]
            mixed = mixed + tap[3] * now
            inputs_out[pl.ds(pl.multiple_of(t * count + (n // 4) * 16, 16), 16), at] = sigmoid_times(mixed).astype(BF)
            for k in range(3):
                kept[k] = jnp.where(acc + k == t + 3, now, kept[k])
            window = [window[1], window[2], now]
        for k in range(3):
            fresh[k, rows, at] = kept[k]
        return 0

    lax.fori_loop(0, (count // 16) * (width // 256), mix, 0)
    sums = lax.dot_general(
        proj[...], inputs_out[...], (((0,), (1,)), ((), ())), preferred_element_type=F32
    )
    sums_out[...] = sums[: sums_out.shape[0]]
    dt_wide[...] = dt_raw[...].astype(F32)
    for c in range(width // 128):
        dt_out[:, c * 128 : (c + 1) * 128] = dt_wide[pl.ds(c, 128, stride=8), :].astype(BF)
    pool_out[...] = pool[...]

    def settle(r, _):
        slot = lax.rem(pages[r], slots)
        for k in range(3):
            pool_out[k, pl.ds(slot, 1), :] = fresh[k, pl.ds(r, 1), :]
        return 0

    lax.fori_loop(0, count, settle, 0)


def scan_kernel(
    pages, accepted, sums_a, sums_b, dt, dt_bias, a_log, inputs, pool, ys_out, kept,
    low, both, delta, decay, start, wide, pick,
):
    tokens, width = inputs.shape
    count = accepted.shape[0]
    drafts = tokens // count
    states = a_log.shape[0]
    rank = low.shape[1]
    slots = pool.shape[0] // states

    def fetch(r, _):
        slot = lax.rem(pages[r], slots)
        for c in range(width // 128):
            start[c, pl.ds(pl.multiple_of(r * states, states), states), :] = pool[
                pl.ds(pl.multiple_of(slot * states, states), states), c * 128 : (c + 1) * 128
            ]
        return 0

    lax.fori_loop(0, count, fetch, 0)
    summed = sums_a[...] + sums_b[...]
    low[...] = summed[:rank].T.astype(BF)
    rest = summed[rank:]
    high = rest.astype(BF).astype(F32)
    middle = (rest - high).astype(BF).astype(F32)
    parts = [high, middle, rest - high - middle, jnp.zeros_like(rest)]
    both[...] = jnp.concatenate(parts, axis=0).T
    row = lax.broadcasted_iota(jnp.int32, (128, 128), 0)
    for q in range(2 * states):
        hit = ((row & (2 * states - 1)) == q) & (row < 6 * states)
        pick[:, q * 128 : (q + 1) * 128] = hit.astype(F32).astype(BF)

    def steps(n, _):
        at = pl.ds(pl.multiple_of(n * 256, 256), 256)
        value = jnp.dot(low[...], dt[:, at], preferred_element_type=F32) + dt_bias[:, at]
        delta[:, at] = jnp.maximum(value, 0.0) + jnp.log1p(jnp.exp(-jnp.abs(value)))
        return 0

    lax.fori_loop(0, width // 256, steps, 0)
    for s in range(states):
        decay[s] = jnp.broadcast_to(-jnp.exp(a_log[s : s + 1, :]) * LOG2E, (8, width))

    def some(rb, _):
        eight = pl.ds(pl.multiple_of(rb * 8, 8), 8)
        terms = jnp.concatenate(
            [both[pl.ds(pl.multiple_of(t * count + rb * 8, 8), 8), :] for t in range(drafts)], axis=0
        ).astype(BF)
        for q in range(0, 2 * states, 4):
            spread = jnp.dot(terms, pick[:, q * 128 : (q + 4) * 128], preferred_element_type=F32)
            for p in range(4):
                wide[:, q + p] = spread[:, p * 128 : (p + 1) * 128].reshape(drafts, 8, 128)
        last = accepted[eight, :] - 1

        def columns(cb, _):
            at = pl.ds(pl.multiple_of(cb * 128, 128), 128)
            first = tuple(
                start[cb, pl.ds(rb * 8 * states + s, 8, stride=states), :] for s in range(states)
            )

            def advance(t, state):
                rows = pl.ds(pl.multiple_of(t * count + rb * 8, 8), 8)
                d = delta[rows, at]
                drive = d * inputs[rows, at].astype(F32)
                here = last == t
                out = None
                nexts = []
                for s in range(states):
                    new = jnp.exp2(d * decay[s, :, at]) * state[s] + drive * wide[t, s]
                    term = new * wide[t, states + s]
                    out = term if out is None else out + term
                    pltpu.store(kept.at[cb, pl.ds(pl.multiple_of(s * count + rb * 8, 8), 8), :], new, mask=here)
                    nexts.append(new)
                ys_out[rows, at] = out
                return tuple(nexts)

            lax.fori_loop(0, drafts, advance, first, unroll=4)
            return 0

        lax.fori_loop(0, width // 128, columns, 0)
        return 0

    lax.fori_loop(0, count // 8, some, 0)


def settle_kernel(pages, kept, pool, pool_out):
    chunks, rows, _ = kept.shape
    count = pages.shape[0]
    states = rows // count
    slots = pool.shape[0] // states

    def carry_over(n, _):
        at = pl.ds(pl.multiple_of(n * states, states), states)
        pool_out[at, :] = pool[at, :]
        return 0

    lax.fori_loop(0, slots, carry_over, 0)

    def settle(r, _):
        slot = lax.rem(pages[r], slots)
        for c in range(chunks):
            for s in range(0, states, 8):
                pool_out[
                    pl.ds(pl.multiple_of(slot * states + s, 8), 8), c * 128 : (c + 1) * 128
                ] = kept[c, pl.ds(s * count + r, 8, stride=count), :]
        return 0

    lax.fori_loop(0, count, settle, 0)


def gate_kernel(
    where, normed, inputs, ys, skip, a0, a1, a2, a3, a4, b0, b1, b2, b3, b4,
    send_out, keep_out, weight, outer, gated, sems,
):
    m = where[1]
    tokens, width = gated.shape
    half = width // 2
    a, b = (a0, a1, a2, a3, a4), (b0, b1, b2, b3, b4)

    def take(src, d, column):
        pltpu.make_async_copy(
            src.at[pl.ds(0, 32), :], weight.at[pl.ds(d * 32, 32), pl.ds(column, half)], sems.at[0]
        ).start()
        pltpu.make_async_copy(
            src.at[pl.ds(32, 32), :], outer.at[pl.ds(d * 32, 32), pl.ds(column, half)], sems.at[1]
        ).start()

    start_pieces(a, place_of(where), True, lambda src, d: take(src, d, 0))
    start_pieces(b, place_of(where), False, lambda src, d: take(src, d, half))
    pltpu.make_async_copy(weight, weight, sems.at[0]).wait()

    def gate(n, _):
        at = pl.ds(pl.multiple_of(n * 256, 256), 256)
        total = jnp.zeros((tokens, 256), F32)
        for k in range(4):
            total = total + jnp.dot(
                normed[k], weight[pl.ds((m ^ k) * 512, 512), at], preferred_element_type=F32
            )
        gates = total.astype(BF).astype(F32)
        mixed = ys[:, at] + skip[:, at] * inputs[:, at].astype(F32)
        gated[:, at] = (mixed * sigmoid_times(gates)).astype(BF)
        return 0

    lax.fori_loop(0, width // 256, gate, 0)
    pltpu.make_async_copy(outer, outer, sems.at[1]).wait()

    def out(part, _):
        column = pl.ds(pl.multiple_of((part & 1) * 256, 256), 256)
        for core in range(2):
            block = m ^ ((part & 2) + core)
            rows = outer[pl.ds(pl.multiple_of(block * 512 + (part & 1) * 256, 256), 256), :]
            value = lax.dot_general(
                gated[...], rows, (((1,), (1,)), ((), ())), preferred_element_type=F32
            )
            if core:
                send_out[part >> 1, :, column] = value.astype(BF)
            else:
                keep_out[part >> 1, :, column] = value
        return 0

    lax.fori_loop(0, 4, out, 0)


def join_kernel(targets, keep, near, far, hidden, out, total):
    tokens, width = hidden.shape
    count = targets.shape[0]
    drafts = tokens // count
    order = order_matrix(tokens, tokens, drafts, count)
    base = jnp.dot(order, hidden[...], preferred_element_type=F32)
    summed = keep[0] + near[0].astype(F32) + far[...].astype(F32)
    rounded = (summed + base).astype(BF)
    back = lax.dot_general(order, rounded, (((0,), (0,)), ((), ())), preferred_element_type=F32)
    total[...] = back.astype(BF).reshape(count, drafts, width)
    out[...] = jnp.zeros(out.shape, BF)

    def place(r, _):
        out[lax.div(targets[r], count)] = total[r]
        return 0

    lax.fori_loop(0, count, place, 0)


def unpack_kernel(where, targets, got, out):
    count = targets.shape[0]
    peers = got.shape[0]

    def take(r, _):
        source = lax.rem(2 * where[0] - lax.div(targets[r], count) + 2 * peers, peers)
        out[r] = got[source]
        return 0

    lax.fori_loop(0, count, take, 0)


def params():
    return pltpu.CompilerParams(vmem_limit_bytes=56 << 20)


def on_device(
    hidden, norm_gain, in_x, in_z, conv_weight, conv_bias, x_proj, dt_proj, dt_bias, a_log, skip,
    out_proj, state_pool, conv_pool, permutation, page_table, accepted,
):
    count, drafts, part = hidden.shape
    tokens = count * drafts
    width = in_x.shape[1]
    slots, states, _ = state_pool.shape
    rank = x_proj.shape[1] - 2 * states
    where = jnp.stack([lax.axis_index("dp"), lax.axis_index("mp")]).astype(jnp.int32)
    peers = lax.axis_size("dp")

    extra = jnp.concatenate(
        [
            x_proj,
            jnp.zeros((16, 256 - x_proj.shape[1]), BF),
            dt_proj.reshape(16, 128),
            jnp.zeros((16, width - CUT), BF),
        ],
        axis=1,
    )
    first = direct(jnp.concatenate([in_x, extra], axis=0), 0)
    middle_a = direct(first[:, :, :CUT], 2)
    middle_b = direct(first[:, :32, CUT:], 1)
    sides_a, sides_b = ring_one(middle_a, 1), ring_one(middle_b, 2)
    first_a = ring_two(middle_a, 1, sides_a)
    first_b = ring_two(middle_b, 2, sides_b)

    flat = hidden.reshape(tokens, part)
    sent = jnp.concatenate([flat, jnp.broadcast_to(norm_gain[None], (16, part))], axis=0)
    near = across(sent, 1)
    far = across(sent, 2)
    both = across(far, 1)
    normed = pl.pallas_call(
        prep_kernel,
        out_shape=jax.ShapeDtypeStruct((4, tokens, part), BF),
        in_specs=[VMEM] * 4,
        out_specs=VMEM,
        scratch_shapes=[pltpu.VMEM((4, tokens, part), BF)],
        compiler_params=params(),
        cost_estimate=pl.CostEstimate(flops=1_000_000, bytes_accessed=1 << 10, transcendentals=0),
        name="prep",
    )(sent, near, far, both)

    pair = after(jnp.concatenate([in_z, out_proj.T], axis=0), first)
    stacked = after(direct(pair, 0), middle_a, middle_b, near, far)
    plane_a = after(direct(stacked[..., : width // 2], 2), first_a, first_b, normed)
    plane_b = after(direct(stacked[..., width // 2 :], 1), first_a, first_b, normed)
    around_a, around_b = ring_one(plane_a, 1), ring_one(plane_b, 2)

    wide_accepted = jnp.broadcast_to(accepted[:, None], (count, 128))
    inputs, sums, dt, new_conv = pl.pallas_call(
        front_kernel,
        out_shape=(
            jax.ShapeDtypeStruct((tokens, width), BF),
            jax.ShapeDtypeStruct((rank + 2 * states, tokens), F32),
            jax.ShapeDtypeStruct((rank, width), BF),
            jax.ShapeDtypeStruct((3, slots, width), F32),
        ),
        in_specs=[SMEM, SMEM] + [VMEM] * 2 + [ANY] * 10 + [VMEM] * 3,
        out_specs=(VMEM,) * 4,
        scratch_shapes=[
            pltpu.VMEM((2048, width), BF),
            pltpu.VMEM((1024, 256), BF),
            pltpu.VMEM((1024, 128), BF),
            pltpu.VMEM((1024, 128), F32),
            pltpu.VMEM((drafts, count, width), F32),
            pltpu.VMEM((3, count, width), F32),
            pltpu.VMEM((3, count, width), F32),
            pltpu.SemaphoreType.DMA((3,)),
        ],
        compiler_params=params(),
        cost_estimate=pl.CostEstimate(flops=1_000_000, bytes_accessed=1 << 10, transcendentals=0),
        name="front",
    )(
        where, page_table, wide_accepted, normed, *first_a, *first_b,
        conv_weight, conv_bias[None], conv_pool.transpose(1, 0, 2),
    )

    sums = sums + across(sums, 1)
    other = after(across(sums, 2), around_a, around_b)
    second = (*ring_two(plane_a, 1, around_a), *ring_two(plane_b, 2, around_b))
    ys, kept = pl.pallas_call(
        scan_kernel,
        out_shape=(
            jax.ShapeDtypeStruct((tokens, width), F32),
            jax.ShapeDtypeStruct((width // 128, states * count, 128), F32),
        ),
        in_specs=[SMEM] + [VMEM] * 8,
        out_specs=(VMEM,) * 2,
        scratch_shapes=[
            pltpu.VMEM((tokens, rank), BF),
            pltpu.VMEM((tokens, 128), F32),
            pltpu.VMEM((tokens, width), F32),
            pltpu.VMEM((states, 8, width), F32),
            pltpu.VMEM((width // 128, count * states, 128), F32),
            pltpu.VMEM((drafts, 2 * states, 8, 128), F32),
            pltpu.VMEM((128, 2 * states * 128), BF),
        ],
        compiler_params=params(),
        cost_estimate=pl.CostEstimate(flops=1_000_000, bytes_accessed=1 << 10, transcendentals=0),
        name="scan",
    )(
        page_table, wide_accepted, sums, other, dt, dt_bias[None], a_log, inputs,
        state_pool.reshape(slots * states, width),
    )

    new_state = pl.pallas_call(
        settle_kernel,
        out_shape=jax.ShapeDtypeStruct((slots * states, width), F32),
        in_specs=[SMEM, VMEM, VMEM],
        out_specs=VMEM,
        compiler_params=params(),
        cost_estimate=pl.CostEstimate(flops=1_000_000, bytes_accessed=1 << 10, transcendentals=0),
        name="settle",
    )(page_table, kept, state_pool.reshape(slots * states, width))

    send, keep = pl.pallas_call(
        gate_kernel,
        out_shape=(
            jax.ShapeDtypeStruct((2, tokens, part), BF),
            jax.ShapeDtypeStruct((2, tokens, part), F32),
        ),
        in_specs=[SMEM] + [VMEM] * 4 + [ANY] * 10,
        out_specs=(VMEM,) * 2,
        scratch_shapes=[
            pltpu.VMEM((2048, width), BF),
            pltpu.VMEM((2048, width), BF),
            pltpu.VMEM((tokens, width), BF),
            pltpu.SemaphoreType.DMA((2,)),
        ],
        compiler_params=params(),
        cost_estimate=pl.CostEstimate(flops=1_000_000, bytes_accessed=1 << 10, transcendentals=0),
        name="gate",
    )(where, normed, inputs, ys, skip[None], *second)
    got = across(send, 1)
    remote = across((keep[1] + got[1].astype(F32)).astype(BF), 2)
    packed = pl.pallas_call(
        join_kernel,
        out_shape=jax.ShapeDtypeStruct((peers, drafts, part), BF),
        in_specs=[SMEM] + [VMEM] * 4,
        out_specs=VMEM,
        scratch_shapes=[pltpu.VMEM((count, drafts, part), BF)],
        compiler_params=params(),
        cost_estimate=pl.CostEstimate(flops=1_000_000, bytes_accessed=1 << 10, transcendentals=0),
        name="join",
    )(permutation, keep, got, remote, flat)
    arrived = lax.all_to_all(packed, "dp", split_axis=0, concat_axis=0, tiled=True)
    verified = pl.pallas_call(
        unpack_kernel,
        out_shape=jax.ShapeDtypeStruct((count, drafts, part), BF),
        in_specs=[SMEM, SMEM, VMEM],
        out_specs=VMEM,
        name="unpack",
    )(where, permutation, arrived)
    return (
        verified,
        new_state.reshape(slots, states, width),
        new_conv.transpose(1, 0, 2),
    )


def solution(mesh):
    return jax.shard_map(
        on_device,
        mesh=mesh,
        in_specs=(
            P("dp", None, "mp"),
            P("mp"),
            P("dp", "mp"),
            P("dp", "mp"),
            P(None, "mp"),
            P("mp"),
            P(("mp", "dp"), None),
            P("dp", "mp"),
            P("mp"),
            P(None, "mp"),
            P("mp"),
            P("mp", "dp"),
            P("dp", None, "mp"),
            P("dp", None, "mp"),
            P("dp"),
            P("dp"),
            P("dp"),
        ),
        out_specs=(P("dp", None, "mp"), P("dp", None, "mp"), P("dp", None, "mp")),
        check_vma=False,
    )
```

```python
import jax
import jax.numpy as jnp
from jax import lax
from jax.experimental import pallas as pl
from jax.experimental.pallas import tpu as pltpu
from jax.sharding import PartitionSpec as P

EPS = 1e-05
LOG2E = 1.4426950408889634
BF = jnp.bfloat16
F32 = jnp.float32
SIDE = 4
CUT = 384

VMEM = pl.BlockSpec(memory_space=pltpu.VMEM)
SMEM = pl.BlockSpec(memory_space=pltpu.SMEM)
ANY = pl.BlockSpec(memory_space=pl.ANY)


def shift_pairs(axis, step):
    pairs = []
    for z in range(SIDE):
        for y in range(SIDE):
            for x in range(SIDE):
                to = [z, y, x]
                to[axis] = (to[axis] + step) % SIDE
                pairs.append(((z * SIDE + y) * SIDE + x, (to[0] * SIDE + to[1]) * SIDE + to[2]))
    return pairs


def hop(value, axis, step):
    return lax.ppermute(value, "dp", shift_pairs(axis, step))


def across(value, flip):
    return lax.ppermute(value, "mp", [(m, m ^ flip) for m in range(4)])


def after(value, *others):
    return lax.optimization_barrier((value, others))[0]


def ring_one(block, axis):
    return hop(block, axis, -1), hop(block, axis, 1)


def ring_two(block, axis, sides):
    half = block.shape[0] // 2
    above, below = sides
    return block, above, hop(below[:half], axis, 1), hop(above[half:], axis, -1), below


def send_direct(block, axis):
    return block, hop(block, axis, -1), hop(block, axis, 2), hop(block, axis, 1)


def exchange_z(block):
    groups = [[z * SIDE * SIDE + i for z in range(SIDE)] for i in range(SIDE * SIDE)]
    many = jnp.broadcast_to(block[None], (SIDE, *block.shape))
    return lax.all_to_all(many, "dp", 0, 0, tiled=True, axis_index_groups=groups)


def direct(block, axis):
    return jnp.stack(send_direct(block, axis))


def start_pieces(pieces, place, middle_first, body, ordered=False):
    z, y, x = place
    own, above, low, high, below = pieces

    def one(n, _):
        i, k = n >> 2, n & 3
        dz = k if ordered else (z + k) & 3

        def piece(f, ref, at):
            if middle_first:
                dx, dy = (x + i) & 3, (y + f) & 3
            else:
                dy, dx = (y + i) & 3, (x + f) & 3
            body(ref.at[at, k], (dz * SIDE + dy) * SIDE + dx)

        piece(0, own, i)
        piece(1, above, i)
        piece(3, below, i)

        @pl.when(i < 2)
        def _():
            piece(2, low, i)

        @pl.when(i >= 2)
        def _():
            piece(2, high, i - 2)

        return 0

    lax.fori_loop(0, SIDE * SIDE, one, 0)


def place_of(where):
    d = where[0]
    return d >> 4, (d >> 2) & 3, d & 3


def sigmoid_times(value):
    return value / (1.0 + jnp.exp(-value))


def order_matrix(rows, columns, drafts, count):
    i = lax.broadcasted_iota(jnp.int32, (rows, columns), 0)
    j = lax.broadcasted_iota(jnp.int32, (rows, columns), 1)
    return ((i % count) * drafts + i // count == j).astype(BF)


def prep_kernel(h0, h1, h2, h3, normed_out, plain):
    tokens = normed_out.shape[1]
    count = 32
    blocks = (h0, h1, h2, h3)
    step = 32

    def norm(n, _):
        at = pl.ds(pl.multiple_of(n * step, step), step)
        rows = [h[at, :].astype(F32) for h in blocks]
        total = sum(jnp.sum(r * r, axis=1, keepdims=True) for r in rows)
        scale = lax.rsqrt(total / (4.0 * rows[0].shape[1]) + EPS)
        for k, h in enumerate(blocks):
            gain = h[pl.ds(tokens, 1), :].astype(F32)
            plain[k, at, :] = (rows[k] * scale * gain).astype(BF)
        return 0

    lax.fori_loop(0, tokens // step, norm, 0)
    order = order_matrix(tokens, tokens, tokens // count, count)
    for k in range(4):
        normed_out[k] = jnp.dot(order, plain[k], preferred_element_type=F32).astype(BF)


def front_kernel(
    where, pages, accepted, normed, a0, a1, a2, a3, a4, b0, b1, b2, b3, b4,
    taps, bias, pool, inputs_out, sums_out, dt_out, pool_out,
    weight, proj, dt_raw, dt_wide, xs, edges, fresh, sems,
):
    place = place_of(where)
    m = where[1]
    drafts, count, width = xs.shape
    tokens = drafts * count
    slots = pool.shape[1]

    def take_a(src, d):
        pltpu.make_async_copy(src.at[pl.ds(0, 32), :], weight.at[pl.ds(d * 32, 32), pl.ds(0, CUT)], sems.at[0]).start()
        pltpu.make_async_copy(src.at[pl.ds(32, 16), pl.ds(0, 256)], proj.at[pl.ds(d * 16, 16), :], sems.at[1]).start()
        pltpu.make_async_copy(src.at[pl.ds(32, 16), pl.ds(256, 128)], dt_raw.at[pl.ds(d * 16, 16), :], sems.at[2]).start()

    def take_b(src, d):
        pltpu.make_async_copy(src, weight.at[pl.ds(d * 32, 32), pl.ds(CUT, width - CUT)], sems.at[0]).start()

    start_pieces((a0, a1, a2, a3, a4), place, True, take_a)
    start_pieces((b0, b1, b2, b3, b4), place, False, take_b)

    def edge(r, _):
        slot = lax.rem(pages[r], slots)
        for k in range(3):
            edges[k, pl.ds(r, 1), :] = pool[k, pl.ds(slot, 1), :]
        return 0

    lax.fori_loop(0, count, edge, 0)
    pltpu.make_async_copy(weight, weight, sems.at[0]).wait()
    pltpu.make_async_copy(proj, proj, sems.at[1]).wait()
    pltpu.make_async_copy(dt_raw, dt_raw, sems.at[2]).wait()

    def project(n, _):
        at = pl.ds(pl.multiple_of(n * 256, 256), 256)
        total = jnp.zeros((tokens, 256), F32)
        for k in range(4):
            total = total + jnp.dot(
                normed[k], weight[pl.ds((m ^ k) * 512, 512), at], preferred_element_type=F32
            )
        xs[:, :, at] = total.astype(BF).astype(F32).reshape(drafts, count, 256)
        return 0

    lax.fori_loop(0, width // 256, project, 0)

    def mix(n, _):
        rows = pl.ds(pl.multiple_of((n // 4) * 16, 16), 16)
        at = pl.ds(pl.multiple_of((n % 4) * 256, 256), 256)
        acc = jnp.concatenate([accepted[rows, :]] * 2, axis=1)
        window = [edges[k, rows, at] for k in range(3)]
        kept = [window[0], window[0], window[0]]
        for p in range(1, 3):
            for k in range(3):
                kept[k] = jnp.where(acc + k == p, window[p], kept[k])
        tap = [taps[k : k + 1, at] for k in range(4)]
        base = bias[:, at]
        for t in range(drafts):
            now = xs[t, rows, at]
            mixed = base + tap[0] * window[0]
            mixed = mixed + tap[1] * window[1]
            mixed = mixed + tap[2] * window[2]
            mixed = mixed + tap[3] * now
            inputs_out[pl.ds(pl.multiple_of(t * count + (n // 4) * 16, 16), 16), at] = sigmoid_times(mixed).astype(BF)
            for k in range(3):
                kept[k] = jnp.where(acc + k == t + 3, now, kept[k])
            window = [window[1], window[2], now]
        for k in range(3):
            fresh[k, rows, at] = kept[k]
        return 0

    lax.fori_loop(0, (count // 16) * (width // 256), mix, 0)
    sums = lax.dot_general(
        proj[...], inputs_out[...], (((0,), (1,)), ((), ())), preferred_element_type=F32
    )
    sums_out[...] = sums[: sums_out.shape[0]]
    dt_wide[...] = dt_raw[...].astype(F32)
    for c in range(width // 128):
        dt_out[:, c * 128 : (c + 1) * 128] = dt_wide[pl.ds(c, 128, stride=8), :].astype(BF)
    pool_out[...] = pool[...]

    def settle(r, _):
        slot = lax.rem(pages[r], slots)
        for k in range(3):
            pool_out[k, pl.ds(slot, 1), :] = fresh[k, pl.ds(r, 1), :]
        return 0

    lax.fori_loop(0, count, settle, 0)


def scan_kernel(
    pages, accepted, sums_a, sums_b, dt, dt_bias, a_log, inputs, pool, ys_out, kept,
    low, both, delta, decay, start, wide, pick,
):
    tokens, width = inputs.shape
    count = accepted.shape[0]
    drafts = tokens // count
    states = a_log.shape[0]
    rank = low.shape[1]
    slots = pool.shape[0] // states

    def fetch(r, _):
        slot = lax.rem(pages[r], slots)
        for c in range(width // 128):
            start[c, pl.ds(pl.multiple_of(r * states, states), states), :] = pool[
                pl.ds(pl.multiple_of(slot * states, states), states), c * 128 : (c + 1) * 128
            ]
        return 0

    lax.fori_loop(0, count, fetch, 0)
    summed = sums_a[...] + sums_b[...]
    low[...] = summed[:rank].T.astype(BF)
    rest = summed[rank:]
    high = rest.astype(BF).astype(F32)
    middle = (rest - high).astype(BF).astype(F32)
    parts = [high, middle, rest - high - middle, jnp.zeros_like(rest)]
    both[...] = jnp.concatenate(parts, axis=0).T
    row = lax.broadcasted_iota(jnp.int32, (128, 128), 0)
    for q in range(2 * states):
        hit = ((row & (2 * states - 1)) == q) & (row < 6 * states)
        pick[:, q * 128 : (q + 1) * 128] = hit.astype(F32).astype(BF)

    def steps(n, _):
        at = pl.ds(pl.multiple_of(n * 256, 256), 256)
        value = jnp.dot(low[...], dt[:, at], preferred_element_type=F32) + dt_bias[:, at]
        delta[:, at] = jnp.maximum(value, 0.0) + jnp.log1p(jnp.exp(-jnp.abs(value)))
        return 0

    lax.fori_loop(0, width // 256, steps, 0)
    for s in range(states):
        decay[s] = jnp.broadcast_to(-jnp.exp(a_log[s : s + 1, :]) * LOG2E, (8, width))

    def some(rb, _):
        eight = pl.ds(pl.multiple_of(rb * 8, 8), 8)
        terms = jnp.concatenate(
            [both[pl.ds(pl.multiple_of(t * count + rb * 8, 8), 8), :] for t in range(drafts)], axis=0
        ).astype(BF)
        for q in range(0, 2 * states, 4):
            spread = jnp.dot(terms, pick[:, q * 128 : (q + 4) * 128], preferred_element_type=F32)
            for p in range(4):
                wide[:, q + p] = spread[:, p * 128 : (p + 1) * 128].reshape(drafts, 8, 128)
        last = accepted[eight, :] - 1

        def columns(cb, _):
            at = pl.ds(pl.multiple_of(cb * 128, 128), 128)
            first = tuple(
                start[cb, pl.ds(rb * 8 * states + s, 8, stride=states), :] for s in range(states)
            )

            def advance(t, state):
                rows = pl.ds(pl.multiple_of(t * count + rb * 8, 8), 8)
                d = delta[rows, at]
                drive = d * inputs[rows, at].astype(F32)
                here = last == t
                out = None
                nexts = []
                for s in range(states):
                    new = jnp.exp2(d * decay[s, :, at]) * state[s] + drive * wide[t, s]
                    term = new * wide[t, states + s]
                    out = term if out is None else out + term
                    pltpu.store(kept.at[cb, pl.ds(pl.multiple_of(s * count + rb * 8, 8), 8), :], new, mask=here)
                    nexts.append(new)
                ys_out[rows, at] = out
                return tuple(nexts)

            lax.fori_loop(0, drafts, advance, first, unroll=4)
            return 0

        lax.fori_loop(0, width // 128, columns, 0)
        return 0

    lax.fori_loop(0, count // 8, some, 0)


def settle_kernel(pages, kept, pool, pool_out):
    chunks, rows, _ = kept.shape
    count = pages.shape[0]
    states = rows // count
    slots = pool.shape[0] // states

    def carry_over(n, _):
        at = pl.ds(pl.multiple_of(n * states, states), states)
        pool_out[at, :] = pool[at, :]
        return 0

    lax.fori_loop(0, slots, carry_over, 0)

    def settle(r, _):
        slot = lax.rem(pages[r], slots)
        for c in range(chunks):
            for s in range(0, states, 8):
                pool_out[
                    pl.ds(pl.multiple_of(slot * states + s, 8), 8), c * 128 : (c + 1) * 128
                ] = kept[c, pl.ds(s * count + r, 8, stride=count), :]
        return 0

    lax.fori_loop(0, count, settle, 0)


def gate_kernel(
    where, normed, inputs, ys, skip, a0, a1, a2, a3, a4, b0, b1, b2, b3, b4,
    send_out, keep_out, weight, outer, gated, sems,
):
    m = where[1]
    tokens, width = gated.shape
    half = width // 2
    a, b = (a0, a1, a2, a3, a4), (b0, b1, b2, b3, b4)

    def take(src, d, column):
        pltpu.make_async_copy(
            src.at[pl.ds(0, 32), :], weight.at[pl.ds(d * 32, 32), pl.ds(column, half)], sems.at[0]
        ).start()
        pltpu.make_async_copy(
            src.at[pl.ds(32, 32), :], outer.at[pl.ds(d * 32, 32), pl.ds(column, half)], sems.at[1]
        ).start()

    start_pieces(a, place_of(where), True, lambda src, d: take(src, d, 0), True)
    start_pieces(b, place_of(where), False, lambda src, d: take(src, d, half), True)
    pltpu.make_async_copy(weight, weight, sems.at[0]).wait()

    def gate(n, _):
        at = pl.ds(pl.multiple_of(n * 256, 256), 256)
        total = jnp.zeros((tokens, 256), F32)
        for k in range(4):
            total = total + jnp.dot(
                normed[k], weight[pl.ds((m ^ k) * 512, 512), at], preferred_element_type=F32
            )
        gates = total.astype(BF).astype(F32)
        mixed = ys[:, at] + skip[:, at] * inputs[:, at].astype(F32)
        gated[:, at] = (mixed * sigmoid_times(gates)).astype(BF)
        return 0

    lax.fori_loop(0, width // 256, gate, 0)
    pltpu.make_async_copy(outer, outer, sems.at[1]).wait()

    def out(part, _):
        column = pl.ds(pl.multiple_of((part & 1) * 256, 256), 256)
        for core in range(2):
            block = m ^ ((part & 2) + core)
            rows = outer[pl.ds(pl.multiple_of(block * 512 + (part & 1) * 256, 256), 256), :]
            value = lax.dot_general(
                gated[...], rows, (((1,), (1,)), ((), ())), preferred_element_type=F32
            )
            if core:
                send_out[part >> 1, :, column] = value.astype(BF)
            else:
                keep_out[part >> 1, :, column] = value
        return 0

    lax.fori_loop(0, 4, out, 0)


def join_kernel(targets, keep, near, far, hidden, out, total):
    tokens, width = hidden.shape
    count = targets.shape[0]
    drafts = tokens // count
    order = order_matrix(tokens, tokens, drafts, count)
    base = jnp.dot(order, hidden[...], preferred_element_type=F32)
    summed = keep[0] + near[0].astype(F32) + far[...].astype(F32)
    rounded = (summed + base).astype(BF)
    back = lax.dot_general(order, rounded, (((0,), (0,)), ((), ())), preferred_element_type=F32)
    total[...] = back.astype(BF).reshape(count, drafts, width)
    out[...] = jnp.zeros(out.shape, BF)

    def place(r, _):
        out[lax.div(targets[r], count)] = total[r]
        return 0

    lax.fori_loop(0, count, place, 0)


def unpack_kernel(where, targets, got, out):
    count = targets.shape[0]
    peers = got.shape[0]

    def take(r, _):
        source = lax.rem(2 * where[0] - lax.div(targets[r], count) + 2 * peers, peers)
        out[r] = got[source]
        return 0

    lax.fori_loop(0, count, take, 0)


def params():
    return pltpu.CompilerParams(vmem_limit_bytes=56 << 20)


def on_device(
    hidden, norm_gain, in_x, in_z, conv_weight, conv_bias, x_proj, dt_proj, dt_bias, a_log, skip,
    out_proj, state_pool, conv_pool, permutation, page_table, accepted,
):
    count, drafts, part = hidden.shape
    tokens = count * drafts
    width = in_x.shape[1]
    slots, states, _ = state_pool.shape
    rank = x_proj.shape[1] - 2 * states
    where = jnp.stack([lax.axis_index("dp"), lax.axis_index("mp")]).astype(jnp.int32)
    peers = lax.axis_size("dp")

    extra = jnp.concatenate(
        [
            x_proj,
            jnp.zeros((16, 256 - x_proj.shape[1]), BF),
            dt_proj.reshape(16, 128),
            jnp.zeros((16, width - CUT), BF),
        ],
        axis=1,
    )
    first = direct(jnp.concatenate([in_x, extra], axis=0), 0)
    middle_a = direct(first[:, :, :CUT], 2)
    middle_b = direct(first[:, :32, CUT:], 1)
    sides_a, sides_b = ring_one(middle_a, 1), ring_one(middle_b, 2)
    first_a = ring_two(middle_a, 1, sides_a)
    first_b = ring_two(middle_b, 2, sides_b)

    flat = hidden.reshape(tokens, part)
    sent = jnp.concatenate([flat, jnp.broadcast_to(norm_gain[None], (16, part))], axis=0)
    sent = after(sent, first)
    near = across(sent, 1)
    far = across(sent, 2)
    both = across(far, 1)
    normed = pl.pallas_call(
        prep_kernel,
        out_shape=jax.ShapeDtypeStruct((4, tokens, part), BF),
        in_specs=[VMEM] * 4,
        out_specs=VMEM,
        scratch_shapes=[pltpu.VMEM((4, tokens, part), BF)],
        compiler_params=params(),
        cost_estimate=pl.CostEstimate(flops=1_000_000, bytes_accessed=1 << 10, transcendentals=0),
        name="prep",
    )(sent, *after((near, far, both), sides_a, sides_b))

    pair = after(jnp.concatenate([in_z, out_proj.T], axis=0), middle_a, middle_b)
    stacked = after(exchange_z(pair), sides_a, sides_b, normed)
    plane_a = send_direct(stacked[..., : width // 2], 2)
    plane_b = send_direct(stacked[..., width // 2 :], 1)

    wide_accepted = jnp.broadcast_to(accepted[:, None], (count, 128))
    inputs, sums, dt, new_conv = pl.pallas_call(
        front_kernel,
        out_shape=(
            jax.ShapeDtypeStruct((tokens, width), BF),
            jax.ShapeDtypeStruct((rank + 2 * states, tokens), F32),
            jax.ShapeDtypeStruct((rank, width), BF),
            jax.ShapeDtypeStruct((3, slots, width), F32),
        ),
        in_specs=[SMEM, SMEM] + [VMEM] * 2 + [ANY] * 10 + [VMEM] * 3,
        out_specs=(VMEM,) * 4,
        scratch_shapes=[
            pltpu.VMEM((2048, width), BF),
            pltpu.VMEM((1024, 256), BF),
            pltpu.VMEM((1024, 128), BF),
            pltpu.VMEM((1024, 128), F32),
            pltpu.VMEM((drafts, count, width), F32),
            pltpu.VMEM((3, count, width), F32),
            pltpu.VMEM((3, count, width), F32),
            pltpu.SemaphoreType.DMA((3,)),
        ],
        compiler_params=params(),
        cost_estimate=pl.CostEstimate(flops=12_000_000_000, bytes_accessed=1 << 10, transcendentals=0),
        name="front",
    )(
        where, page_table, wide_accepted, normed, *first_a, *first_b,
        conv_weight, conv_bias[None], conv_pool.transpose(1, 0, 2),
    )

    plane_a, plane_b = (jnp.stack(p) for p in after((plane_a, plane_b), sums))
    around_a, around_b = ring_one(plane_a, 1), ring_one(plane_b, 2)
    sums = sums + across(sums, 1)
    other = across(sums, 2)
    ys, kept = pl.pallas_call(
        scan_kernel,
        out_shape=(
            jax.ShapeDtypeStruct((tokens, width), F32),
            jax.ShapeDtypeStruct((width // 128, states * count, 128), F32),
        ),
        in_specs=[SMEM] + [VMEM] * 8,
        out_specs=(VMEM,) * 2,
        scratch_shapes=[
            pltpu.VMEM((tokens, rank), BF),
            pltpu.VMEM((tokens, 128), F32),
            pltpu.VMEM((tokens, width), F32),
            pltpu.VMEM((states, 8, width), F32),
            pltpu.VMEM((width // 128, count * states, 128), F32),
            pltpu.VMEM((drafts, 2 * states, 8, 128), F32),
            pltpu.VMEM((128, 2 * states * 128), BF),
        ],
        compiler_params=params(),
        cost_estimate=pl.CostEstimate(flops=1_000_000, bytes_accessed=1 << 10, transcendentals=0),
        name="scan",
    )(
        page_table, wide_accepted, sums, other, dt, dt_bias[None], a_log, inputs,
        state_pool.reshape(slots * states, width),
    )

    around_a, around_b = after((around_a, around_b), ys)
    second = (*ring_two(plane_a, 1, around_a), *ring_two(plane_b, 2, around_b))
    new_state = pl.pallas_call(
        settle_kernel,
        out_shape=jax.ShapeDtypeStruct((slots * states, width), F32),
        in_specs=[SMEM, VMEM, VMEM],
        out_specs=VMEM,
        compiler_params=params(),
        cost_estimate=pl.CostEstimate(flops=1_000_000, bytes_accessed=1 << 10, transcendentals=0),
        name="settle",
    )(page_table, kept, state_pool.reshape(slots * states, width))

    send, keep = pl.pallas_call(
        gate_kernel,
        out_shape=(
            jax.ShapeDtypeStruct((2, tokens, part), BF),
            jax.ShapeDtypeStruct((2, tokens, part), F32),
        ),
        in_specs=[SMEM] + [VMEM] * 4 + [ANY] * 10,
        out_specs=(VMEM,) * 2,
        scratch_shapes=[
            pltpu.VMEM((2048, width), BF),
            pltpu.VMEM((2048, width), BF),
            pltpu.VMEM((tokens, width), BF),
            pltpu.SemaphoreType.DMA((2,)),
        ],
        compiler_params=params(),
        cost_estimate=pl.CostEstimate(flops=1_000_000, bytes_accessed=1 << 10, transcendentals=0),
        name="gate",
    )(where, normed, inputs, ys, skip[None], *second)
    got = across(send, 1)
    remote = across((keep[1] + got[1].astype(F32)).astype(BF), 2)
    packed = pl.pallas_call(
        join_kernel,
        out_shape=jax.ShapeDtypeStruct((peers, drafts, part), BF),
        in_specs=[SMEM] + [VMEM] * 4,
        out_specs=VMEM,
        scratch_shapes=[pltpu.VMEM((count, drafts, part), BF)],
        compiler_params=params(),
        cost_estimate=pl.CostEstimate(flops=1_000_000, bytes_accessed=1 << 10, transcendentals=0),
        name="join",
    )(permutation, keep, got, remote, flat)
    arrived = lax.all_to_all(packed, "dp", split_axis=0, concat_axis=0, tiled=True)
    verified = pl.pallas_call(
        unpack_kernel,
        out_shape=jax.ShapeDtypeStruct((count, drafts, part), BF),
        in_specs=[SMEM, SMEM, VMEM],
        out_specs=VMEM,
        name="unpack",
    )(where, permutation, arrived)
    return (
        verified,
        new_state.reshape(slots, states, width),
        new_conv.transpose(1, 0, 2),
    )


def solution(mesh):
    return jax.shard_map(
        on_device,
        mesh=mesh,
        in_specs=(
            P("dp", None, "mp"),
            P("mp"),
            P("dp", "mp"),
            P("dp", "mp"),
            P(None, "mp"),
            P("mp"),
            P(("mp", "dp"), None),
            P("dp", "mp"),
            P("mp"),
            P(None, "mp"),
            P("mp"),
            P("mp", "dp"),
            P("dp", None, "mp"),
            P("dp", None, "mp"),
            P("dp"),
            P("dp"),
            P("dp"),
        ),
        out_specs=(P("dp", None, "mp"), P("dp", None, "mp"), P("dp", None, "mp")),
        check_vma=False,
    )
```

```python
import jax
import jax.numpy as jnp
from jax import lax
from jax.experimental import pallas as pl
from jax.experimental.pallas import tpu as pltpu
from jax.sharding import PartitionSpec as P

EPS = 1e-05
LOG2E = 1.4426950408889634
BF = jnp.bfloat16
F32 = jnp.float32
SIDE = 4
CUT = 384

VMEM = pl.BlockSpec(memory_space=pltpu.VMEM)
SMEM = pl.BlockSpec(memory_space=pltpu.SMEM)
ANY = pl.BlockSpec(memory_space=pl.ANY)


def shift_pairs(axis, step):
    pairs = []
    for z in range(SIDE):
        for y in range(SIDE):
            for x in range(SIDE):
                to = [z, y, x]
                to[axis] = (to[axis] + step) % SIDE
                pairs.append(((z * SIDE + y) * SIDE + x, (to[0] * SIDE + to[1]) * SIDE + to[2]))
    return pairs


def hop(value, axis, step):
    return lax.ppermute(value, "dp", shift_pairs(axis, step))


def across(value, flip):
    return lax.ppermute(value, "mp", [(m, m ^ flip) for m in range(4)])


def after(value, *others):
    return lax.optimization_barrier((value, others))[0]


def ring_one(block, axis):
    return hop(block, axis, -1), hop(block, axis, 1)


def ring_two(block, axis, sides):
    half = block.shape[0] // 2
    above, below = sides
    return block, above, hop(below[:half], axis, 1), hop(above[half:], axis, -1), below


def send_direct(block, axis):
    return block, hop(block, axis, -1), hop(block, axis, 2), hop(block, axis, 1)


def exchange_z(block):
    groups = [[z * SIDE * SIDE + i for z in range(SIDE)] for i in range(SIDE * SIDE)]
    many = jnp.broadcast_to(block[None], (SIDE, *block.shape))
    return lax.all_to_all(many, "dp", 0, 0, tiled=True, axis_index_groups=groups)


def direct(block, axis):
    return jnp.stack(send_direct(block, axis))


def start_pieces(pieces, place, middle_first, body):
    z, y, x = place
    own, above, low, high, below = pieces

    def one(n, _):
        i, k = n >> 2, n & 3
        dz = (z + k) & 3

        def piece(f, ref, at):
            if middle_first:
                dx, dy = (x + i) & 3, (y + f) & 3
            else:
                dy, dx = (y + i) & 3, (x + f) & 3
            body(ref.at[at, k], (dz * SIDE + dy) * SIDE + dx)

        piece(0, own, i)
        piece(1, above, i)
        piece(3, below, i)

        @pl.when(i < 2)
        def _():
            piece(2, low, i)

        @pl.when(i >= 2)
        def _():
            piece(2, high, i - 2)

        return 0

    lax.fori_loop(0, SIDE * SIDE, one, 0)


def place_of(where):
    d = where[0]
    return d >> 4, (d >> 2) & 3, d & 3


def sigmoid_times(value):
    return value / (1.0 + jnp.exp(-value))


def order_matrix(rows, columns, drafts, count):
    i = lax.broadcasted_iota(jnp.int32, (rows, columns), 0)
    j = lax.broadcasted_iota(jnp.int32, (rows, columns), 1)
    return ((i % count) * drafts + i // count == j).astype(BF)


def prep_kernel(h0, h1, h2, h3, normed_out, plain):
    tokens = normed_out.shape[1]
    count = 32
    blocks = (h0, h1, h2, h3)
    step = 32

    def norm(n, _):
        at = pl.ds(pl.multiple_of(n * step, step), step)
        rows = [h[at, :].astype(F32) for h in blocks]
        total = sum(jnp.sum(r * r, axis=1, keepdims=True) for r in rows)
        scale = lax.rsqrt(total / (4.0 * rows[0].shape[1]) + EPS)
        for k, h in enumerate(blocks):
            gain = h[pl.ds(tokens, 1), :].astype(F32)
            plain[k, at, :] = (rows[k] * scale * gain).astype(BF)
        return 0

    lax.fori_loop(0, tokens // step, norm, 0)
    order = order_matrix(tokens, tokens, tokens // count, count)
    for k in range(4):
        normed_out[k] = jnp.dot(order, plain[k], preferred_element_type=F32).astype(BF)


def front_kernel(
    where, pages, accepted, normed, a0, a1, a2, a3, a4, b0, b1, b2, b3, b4,
    taps, bias, pool, inputs_out, sums_out, dt_out, pool_out,
    weight, proj, dt_raw, dt_wide, xs, edges, fresh, sems,
):
    place = place_of(where)
    m = where[1]
    drafts, count, width = xs.shape
    tokens = drafts * count
    slots = pool.shape[1]

    def take_a(src, d):
        pltpu.make_async_copy(src.at[pl.ds(0, 32), :], weight.at[pl.ds(d * 32, 32), pl.ds(0, CUT)], sems.at[0]).start()
        pltpu.make_async_copy(src.at[pl.ds(32, 16), pl.ds(0, 256)], proj.at[pl.ds(d * 16, 16), :], sems.at[1]).start()
        pltpu.make_async_copy(src.at[pl.ds(32, 16), pl.ds(256, 128)], dt_raw.at[pl.ds(d * 16, 16), :], sems.at[2]).start()

    def take_b(src, d):
        pltpu.make_async_copy(src, weight.at[pl.ds(d * 32, 32), pl.ds(CUT, width - CUT)], sems.at[0]).start()

    start_pieces((a0, a1, a2, a3, a4), place, True, take_a)
    start_pieces((b0, b1, b2, b3, b4), place, False, take_b)

    def edge(r, _):
        slot = lax.rem(pages[r], slots)
        for k in range(3):
            edges[k, pl.ds(r, 1), :] = pool[k, pl.ds(slot, 1), :]
        return 0

    lax.fori_loop(0, count, edge, 0)
    pltpu.make_async_copy(weight, weight, sems.at[0]).wait()
    pltpu.make_async_copy(proj, proj, sems.at[1]).wait()
    pltpu.make_async_copy(dt_raw, dt_raw, sems.at[2]).wait()

    def project(n, _):
        at = pl.ds(pl.multiple_of(n * 256, 256), 256)
        total = jnp.zeros((tokens, 256), F32)
        for k in range(4):
            total = total + jnp.dot(
                normed[k], weight[pl.ds((m ^ k) * 512, 512), at], preferred_element_type=F32
            )
        xs[:, :, at] = total.astype(BF).astype(F32).reshape(drafts, count, 256)
        return 0

    lax.fori_loop(0, width // 256, project, 0)

    def mix(n, _):
        rows = pl.ds(pl.multiple_of((n // 4) * 16, 16), 16)
        at = pl.ds(pl.multiple_of((n % 4) * 256, 256), 256)
        acc = jnp.concatenate([accepted[rows, :]] * 2, axis=1)
        window = [edges[k, rows, at] for k in range(3)]
        kept = [window[0], window[0], window[0]]
        for p in range(1, 3):
            for k in range(3):
                kept[k] = jnp.where(acc + k == p, window[p], kept[k])
        tap = [taps[k : k + 1, at] for k in range(4)]
        base = bias[:, at]
        for t in range(drafts):
            now = xs[t, rows, at]
            mixed = base + tap[0] * window[0]
            mixed = mixed + tap[1] * window[1]
            mixed = mixed + tap[2] * window[2]
            mixed = mixed + tap[3] * now
            inputs_out[pl.ds(pl.multiple_of(t * count + (n // 4) * 16, 16), 16), at] = sigmoid_times(mixed).astype(BF)
            for k in range(3):
                kept[k] = jnp.where(acc + k == t + 3, now, kept[k])
            window = [window[1], window[2], now]
        for k in range(3):
            fresh[k, rows, at] = kept[k]
        return 0

    lax.fori_loop(0, (count // 16) * (width // 256), mix, 0)
    sums = lax.dot_general(
        proj[...], inputs_out[...], (((0,), (1,)), ((), ())), preferred_element_type=F32
    )
    sums_out[...] = sums[: sums_out.shape[0]]
    dt_wide[...] = dt_raw[...].astype(F32)
    for c in range(width // 128):
        dt_out[:, c * 128 : (c + 1) * 128] = dt_wide[pl.ds(c, 128, stride=8), :].astype(BF)
    pool_out[...] = pool[...]

    def settle(r, _):
        slot = lax.rem(pages[r], slots)
        for k in range(3):
            pool_out[k, pl.ds(slot, 1), :] = fresh[k, pl.ds(r, 1), :]
        return 0

    lax.fori_loop(0, count, settle, 0)


def scan_kernel(
    pages, accepted, sums_a, sums_b, dt, dt_bias, a_log, inputs, pool, ys_out, kept,
    low, both, delta, decay, start, wide, pick,
):
    tokens, width = inputs.shape
    count = accepted.shape[0]
    drafts = tokens // count
    states = a_log.shape[0]
    rank = low.shape[1]
    slots = pool.shape[0] // states

    def fetch(r, _):
        slot = lax.rem(pages[r], slots)
        for c in range(width // 128):
            start[c, pl.ds(pl.multiple_of(r * states, states), states), :] = pool[
                pl.ds(pl.multiple_of(slot * states, states), states), c * 128 : (c + 1) * 128
            ]
        return 0

    lax.fori_loop(0, count, fetch, 0)
    summed = sums_a[...] + sums_b[...].astype(F32)
    low[...] = summed[:rank].T.astype(BF)
    rest = summed[rank:]
    high = rest.astype(BF).astype(F32)
    middle = (rest - high).astype(BF).astype(F32)
    parts = [high, middle, rest - high - middle, jnp.zeros_like(rest)]
    both[...] = jnp.concatenate(parts, axis=0).T
    row = lax.broadcasted_iota(jnp.int32, (128, 128), 0)
    for q in range(2 * states):
        hit = ((row & (2 * states - 1)) == q) & (row < 6 * states)
        pick[:, q * 128 : (q + 1) * 128] = hit.astype(F32).astype(BF)

    def steps(n, _):
        at = pl.ds(pl.multiple_of(n * 256, 256), 256)
        value = jnp.dot(low[...], dt[:, at], preferred_element_type=F32) + dt_bias[:, at]
        delta[:, at] = jnp.maximum(value, 0.0) + jnp.log1p(jnp.exp(-jnp.abs(value)))
        return 0

    lax.fori_loop(0, width // 256, steps, 0)
    for s in range(states):
        decay[s] = jnp.broadcast_to(-jnp.exp(a_log[s : s + 1, :]) * LOG2E, (8, width))

    def some(rb, _):
        eight = pl.ds(pl.multiple_of(rb * 8, 8), 8)
        terms = jnp.concatenate(
            [both[pl.ds(pl.multiple_of(t * count + rb * 8, 8), 8), :] for t in range(drafts)], axis=0
        ).astype(BF)
        for q in range(0, 2 * states, 4):
            spread = jnp.dot(terms, pick[:, q * 128 : (q + 4) * 128], preferred_element_type=F32)
            for p in range(4):
                wide[:, q + p] = spread[:, p * 128 : (p + 1) * 128].reshape(drafts, 8, 128)
        last = accepted[eight, :] - 1

        def columns(cb, _):
            at = pl.ds(pl.multiple_of(cb * 128, 128), 128)
            first = tuple(
                start[cb, pl.ds(rb * 8 * states + s, 8, stride=states), :] for s in range(states)
            )

            def advance(t, state):
                rows = pl.ds(pl.multiple_of(t * count + rb * 8, 8), 8)
                d = delta[rows, at]
                drive = d * inputs[rows, at].astype(F32)
                here = last == t
                out = None
                nexts = []
                for s in range(states):
                    new = jnp.exp2(d * decay[s, :, at]) * state[s] + drive * wide[t, s]
                    term = new * wide[t, states + s]
                    out = term if out is None else out + term
                    pltpu.store(kept.at[cb, pl.ds(pl.multiple_of(s * count + rb * 8, 8), 8), :], new, mask=here)
                    nexts.append(new)
                ys_out[rows, at] = out
                return tuple(nexts)

            lax.fori_loop(0, drafts, advance, first, unroll=4)
            return 0

        lax.fori_loop(0, width // 128, columns, 0)
        return 0

    lax.fori_loop(0, count // 8, some, 0)


def settle_kernel(pages, kept, pool, pool_out):
    chunks, rows, _ = kept.shape
    count = pages.shape[0]
    states = rows // count
    slots = pool.shape[0] // states

    def carry_over(n, _):
        at = pl.ds(pl.multiple_of(n * states, states), states)
        pool_out[at, :] = pool[at, :]
        return 0

    lax.fori_loop(0, slots, carry_over, 0)

    def settle(r, _):
        slot = lax.rem(pages[r], slots)
        for c in range(chunks):
            for s in range(0, states, 8):
                pool_out[
                    pl.ds(pl.multiple_of(slot * states + s, 8), 8), c * 128 : (c + 1) * 128
                ] = kept[c, pl.ds(s * count + r, 8, stride=count), :]
        return 0

    lax.fori_loop(0, count, settle, 0)


def gate_kernel(
    where, normed, inputs, ys, skip, second, send_out, keep_out, weight, outer, gated, sems
):
    m = where[1]
    tokens, width = gated.shape
    for z in range(SIDE):
        pltpu.make_async_copy(second.at[:, z, pl.ds(0, 32), :], weight.at[z], sems.at[0]).start()
    for z in range(SIDE):
        pltpu.make_async_copy(second.at[:, z, pl.ds(32, 32), :], outer.at[z], sems.at[1]).start()
    pltpu.make_async_copy(weight, weight, sems.at[0]).wait()

    def gate(n, _):
        at = pl.ds(pl.multiple_of(n * 256, 256), 256)
        total = jnp.zeros((tokens, 256), F32)
        for k in range(4):
            block = weight[m ^ k, :, :, at].reshape(512, 256)
            total = total + jnp.dot(normed[k], block, preferred_element_type=F32)
        gates = total.astype(BF).astype(F32)
        mixed = ys[:, at] + skip[:, at] * inputs[:, at].astype(F32)
        gated[:, at] = (mixed * sigmoid_times(gates)).astype(BF)
        return 0

    lax.fori_loop(0, width // 256, gate, 0)
    pltpu.make_async_copy(outer, outer, sems.at[1]).wait()

    def out(part, _):
        column = pl.ds(pl.multiple_of((part & 1) * 256, 256), 256)
        for core in range(2):
            block = m ^ ((part & 2) + core)
            rows = outer[block, pl.ds((part & 1) * 8, 8), :, :].reshape(256, width)
            value = lax.dot_general(
                gated[...], rows, (((1,), (1,)), ((), ())), preferred_element_type=F32
            )
            if core:
                send_out[part >> 1, :, column] = value.astype(BF)
            else:
                keep_out[part >> 1, :, column] = value
        return 0

    lax.fori_loop(0, 4, out, 0)


def join_kernel(targets, keep, near, far, hidden, out, total):
    tokens, width = hidden.shape
    count = targets.shape[0]
    drafts = tokens // count
    order = order_matrix(tokens, tokens, drafts, count)
    base = jnp.dot(order, hidden[...], preferred_element_type=F32)
    summed = keep[0] + near[0].astype(F32) + far[...].astype(F32)
    rounded = (summed + base).astype(BF)
    back = lax.dot_general(order, rounded, (((0,), (0,)), ((), ())), preferred_element_type=F32)
    total[...] = back.astype(BF).reshape(count, drafts, width)
    out[...] = jnp.zeros(out.shape, BF)

    def place(r, _):
        out[lax.div(targets[r], count)] = total[r]
        return 0

    lax.fori_loop(0, count, place, 0)


def unpack_kernel(where, targets, got, out):
    count = targets.shape[0]
    peers = got.shape[0]

    def take(r, _):
        source = lax.rem(2 * where[0] - lax.div(targets[r], count) + 2 * peers, peers)
        out[r] = got[source]
        return 0

    lax.fori_loop(0, count, take, 0)


def params():
    return pltpu.CompilerParams(vmem_limit_bytes=56 << 20)


def on_device(
    hidden, norm_gain, in_x, in_z, conv_weight, conv_bias, x_proj, dt_proj, dt_bias, a_log, skip,
    out_proj, state_pool, conv_pool, permutation, page_table, accepted,
):
    count, drafts, part = hidden.shape
    tokens = count * drafts
    width = in_x.shape[1]
    slots, states, _ = state_pool.shape
    rank = x_proj.shape[1] - 2 * states
    where = jnp.stack([lax.axis_index("dp"), lax.axis_index("mp")]).astype(jnp.int32)
    peers = lax.axis_size("dp")

    extra = jnp.concatenate(
        [
            x_proj,
            jnp.zeros((16, 256 - x_proj.shape[1]), BF),
            dt_proj.reshape(16, 128),
            jnp.zeros((16, width - CUT), BF),
        ],
        axis=1,
    )
    first = direct(jnp.concatenate([in_x, extra], axis=0), 0)
    middle_a = direct(first[:, :, :CUT], 2)
    middle_b = direct(first[:, :32, CUT:], 1)
    middle_a, middle_b = lax.optimization_barrier((middle_a, middle_b))
    sides_a, sides_b = ring_one(middle_a, 1), ring_one(middle_b, 2)
    first_a = ring_two(middle_a, 1, sides_a)
    first_b = ring_two(middle_b, 2, sides_b)

    flat = hidden.reshape(tokens, part)
    sent = jnp.concatenate([flat, jnp.broadcast_to(norm_gain[None], (16, part))], axis=0)
    sent = after(sent, middle_a, middle_b)
    near = across(sent, 1)
    far = across(sent, 2)
    both = across(far, 1)
    normed = pl.pallas_call(
        prep_kernel,
        out_shape=jax.ShapeDtypeStruct((4, tokens, part), BF),
        in_specs=[VMEM] * 4,
        out_specs=VMEM,
        scratch_shapes=[pltpu.VMEM((4, tokens, part), BF)],
        compiler_params=params(),
        cost_estimate=pl.CostEstimate(flops=1_000_000, bytes_accessed=1 << 10, transcendentals=0),
        name="prep",
    )(sent, *after((near, far, both), sides_a, sides_b))

    pair = after(jnp.concatenate([in_z, out_proj.T], axis=0), first)
    second = lax.all_gather(
        exchange_z(pair), "dp", axis=0,
        axis_index_groups=[[z * 16 + i for i in range(16)] for z in range(SIDE)],
    )

    wide_accepted = jnp.broadcast_to(accepted[:, None], (count, 128))
    inputs, sums, dt, new_conv = pl.pallas_call(
        front_kernel,
        out_shape=(
            jax.ShapeDtypeStruct((tokens, width), BF),
            jax.ShapeDtypeStruct((rank + 2 * states, tokens), F32),
            jax.ShapeDtypeStruct((rank, width), BF),
            jax.ShapeDtypeStruct((3, slots, width), F32),
        ),
        in_specs=[SMEM, SMEM] + [VMEM] * 2 + [ANY] * 10 + [VMEM] * 3,
        out_specs=(VMEM,) * 4,
        scratch_shapes=[
            pltpu.VMEM((2048, width), BF),
            pltpu.VMEM((1024, 256), BF),
            pltpu.VMEM((1024, 128), BF),
            pltpu.VMEM((1024, 128), F32),
            pltpu.VMEM((drafts, count, width), F32),
            pltpu.VMEM((3, count, width), F32),
            pltpu.VMEM((3, count, width), F32),
            pltpu.SemaphoreType.DMA((3,)),
        ],
        compiler_params=params(),
        cost_estimate=pl.CostEstimate(flops=12_000_000_000, bytes_accessed=1 << 10, transcendentals=0),
        name="front",
    )(
        where, page_table, wide_accepted, normed, *first_a, *first_b,
        conv_weight, conv_bias[None], conv_pool.transpose(1, 0, 2),
    )

    sums = sums + across(sums, 1)
    other = across(sums.astype(BF), 2)
    ys, kept = pl.pallas_call(
        scan_kernel,
        out_shape=(
            jax.ShapeDtypeStruct((tokens, width), F32),
            jax.ShapeDtypeStruct((width // 128, states * count, 128), F32),
        ),
        in_specs=[SMEM] + [VMEM] * 8,
        out_specs=(VMEM,) * 2,
        scratch_shapes=[
            pltpu.VMEM((tokens, rank), BF),
            pltpu.VMEM((tokens, 128), F32),
            pltpu.VMEM((tokens, width), F32),
            pltpu.VMEM((states, 8, width), F32),
            pltpu.VMEM((width // 128, count * states, 128), F32),
            pltpu.VMEM((drafts, 2 * states, 8, 128), F32),
            pltpu.VMEM((128, 2 * states * 128), BF),
        ],
        compiler_params=params(),
        cost_estimate=pl.CostEstimate(flops=1_000_000, bytes_accessed=1 << 10, transcendentals=0),
        name="scan",
    )(
        page_table, wide_accepted, sums, other, dt, dt_bias[None], a_log, inputs,
        state_pool.reshape(slots * states, width),
    )

    new_state = pl.pallas_call(
        settle_kernel,
        out_shape=jax.ShapeDtypeStruct((slots * states, width), F32),
        in_specs=[SMEM, VMEM, VMEM],
        out_specs=VMEM,
        compiler_params=params(),
        cost_estimate=pl.CostEstimate(flops=1_000_000, bytes_accessed=1 << 10, transcendentals=0),
        name="settle",
    )(page_table, kept, state_pool.reshape(slots * states, width))

    send, keep = pl.pallas_call(
        gate_kernel,
        out_shape=(
            jax.ShapeDtypeStruct((2, tokens, part), BF),
            jax.ShapeDtypeStruct((2, tokens, part), F32),
        ),
        in_specs=[SMEM] + [VMEM] * 4 + [ANY],
        out_specs=(VMEM,) * 2,
        scratch_shapes=[
            pltpu.VMEM((SIDE, 16, 32, width), BF),
            pltpu.VMEM((SIDE, 16, 32, width), BF),
            pltpu.VMEM((tokens, width), BF),
            pltpu.SemaphoreType.DMA((2,)),
        ],
        compiler_params=params(),
        cost_estimate=pl.CostEstimate(flops=1_000_000, bytes_accessed=1 << 10, transcendentals=0),
        name="gate",
    )(where, normed, inputs, ys, skip[None], second)
    got = across(send, 1)
    remote = across((keep[1] + got[1].astype(F32)).astype(BF), 2)
    packed = pl.pallas_call(
        join_kernel,
        out_shape=jax.ShapeDtypeStruct((peers, drafts, part), BF),
        in_specs=[SMEM] + [VMEM] * 4,
        out_specs=VMEM,
        scratch_shapes=[pltpu.VMEM((count, drafts, part), BF)],
        compiler_params=params(),
        cost_estimate=pl.CostEstimate(flops=1_000_000, bytes_accessed=1 << 10, transcendentals=0),
        name="join",
    )(permutation, keep, got, remote, flat)
    arrived = lax.all_to_all(packed, "dp", split_axis=0, concat_axis=0, tiled=True)
    verified = pl.pallas_call(
        unpack_kernel,
        out_shape=jax.ShapeDtypeStruct((count, drafts, part), BF),
        in_specs=[SMEM, SMEM, VMEM],
        out_specs=VMEM,
        name="unpack",
    )(where, permutation, arrived)
    return (
        verified,
        new_state.reshape(slots, states, width),
        new_conv.transpose(1, 0, 2),
    )


def solution(mesh):
    return jax.shard_map(
        on_device,
        mesh=mesh,
        in_specs=(
            P("dp", None, "mp"),
            P("mp"),
            P("dp", "mp"),
            P("dp", "mp"),
            P(None, "mp"),
            P("mp"),
            P(("mp", "dp"), None),
            P("dp", "mp"),
            P("mp"),
            P(None, "mp"),
            P("mp"),
            P("mp", "dp"),
            P("dp", None, "mp"),
            P("dp", None, "mp"),
            P("dp"),
            P("dp"),
            P("dp"),
        ),
        out_specs=(P("dp", None, "mp"), P("dp", None, "mp"), P("dp", None, "mp")),
        check_vma=False,
    )
```

```python
import jax
import jax.numpy as jnp
from jax import lax
from jax.experimental import pallas as pl
from jax.experimental.pallas import tpu as pltpu
from jax.sharding import PartitionSpec as P

EPS = 1e-05
LOG2E = 1.4426950408889634
BF = jnp.bfloat16
F32 = jnp.float32
SIDE = 4
CUT = 384

VMEM = pl.BlockSpec(memory_space=pltpu.VMEM)
SMEM = pl.BlockSpec(memory_space=pltpu.SMEM)
ANY = pl.BlockSpec(memory_space=pl.ANY)


def shift_pairs(axis, step):
    pairs = []
    for z in range(SIDE):
        for y in range(SIDE):
            for x in range(SIDE):
                to = [z, y, x]
                to[axis] = (to[axis] + step) % SIDE
                pairs.append(((z * SIDE + y) * SIDE + x, (to[0] * SIDE + to[1]) * SIDE + to[2]))
    return pairs


def hop(value, axis, step):
    return lax.ppermute(value, "dp", shift_pairs(axis, step))


def across(value, flip):
    return lax.ppermute(value, "mp", [(m, m ^ flip) for m in range(4)])


def after(value, *others):
    return lax.optimization_barrier((value, others))[0]


def ring_one(block, axis):
    return hop(block, axis, -1), hop(block, axis, 1)


def ring_two(block, axis, sides):
    half = block.shape[0] // 2
    above, below = sides
    return block, above, hop(below[:half], axis, 1), hop(above[half:], axis, -1), below


def send_direct(block, axis):
    return block, hop(block, axis, -1), hop(block, axis, 2), hop(block, axis, 1)


def direct(block, axis):
    return jnp.stack(send_direct(block, axis))


def start_pieces(pieces, place, middle_first, body):
    z, y, x = place
    own, above, low, high, below = pieces

    def one(n, _):
        i, k = n >> 2, n & 3
        dz = (z + k) & 3

        def piece(f, ref, at):
            if middle_first:
                dx, dy = (x + i) & 3, (y + f) & 3
            else:
                dy, dx = (y + i) & 3, (x + f) & 3
            body(ref.at[at, k], (dz * SIDE + dy) * SIDE + dx)

        piece(0, own, i)
        piece(1, above, i)
        piece(3, below, i)

        @pl.when(i < 2)
        def _():
            piece(2, low, i)

        @pl.when(i >= 2)
        def _():
            piece(2, high, i - 2)

        return 0

    lax.fori_loop(0, SIDE * SIDE, one, 0)


def place_of(where):
    d = where[0]
    return d >> 4, (d >> 2) & 3, d & 3


def sigmoid_times(value):
    return value / (1.0 + jnp.exp(-value))


def order_matrix(rows, columns, drafts, count):
    i = lax.broadcasted_iota(jnp.int32, (rows, columns), 0)
    j = lax.broadcasted_iota(jnp.int32, (rows, columns), 1)
    return ((i % count) * drafts + i // count == j).astype(BF)


def prep_kernel(h0, h1, h2, h3, normed_out, plain):
    tokens = normed_out.shape[1]
    count = 32
    blocks = (h0, h1, h2, h3)
    step = 32

    def norm(n, _):
        at = pl.ds(pl.multiple_of(n * step, step), step)
        rows = [h[at, :].astype(F32) for h in blocks]
        total = sum(jnp.sum(r * r, axis=1, keepdims=True) for r in rows)
        scale = lax.rsqrt(total / (4.0 * rows[0].shape[1]) + EPS)
        for k, h in enumerate(blocks):
            gain = h[pl.ds(tokens, 1), :].astype(F32)
            plain[k, at, :] = (rows[k] * scale * gain).astype(BF)
        return 0

    lax.fori_loop(0, tokens // step, norm, 0)
    order = order_matrix(tokens, tokens, tokens // count, count)
    for k in range(4):
        normed_out[k] = jnp.dot(order, plain[k], preferred_element_type=F32).astype(BF)


def front_kernel(
    where, pages, accepted, normed, a0, a1, a2, a3, a4, b0, b1, b2, b3, b4,
    taps, bias, pool, inputs_out, sums_out, dt_out, pool_out,
    weight, proj, dt_raw, dt_wide, xs, edges, fresh, sems,
):
    place = place_of(where)
    m = where[1]
    drafts, count, width = xs.shape
    tokens = drafts * count
    slots = pool.shape[1]

    def take_a(src, d):
        pltpu.make_async_copy(src.at[pl.ds(0, 32), :], weight.at[pl.ds(d * 32, 32), pl.ds(0, CUT)], sems.at[0]).start()
        pltpu.make_async_copy(src.at[pl.ds(32, 16), pl.ds(0, 256)], proj.at[pl.ds(d * 16, 16), :], sems.at[1]).start()
        pltpu.make_async_copy(src.at[pl.ds(32, 16), pl.ds(256, 128)], dt_raw.at[pl.ds(d * 16, 16), :], sems.at[2]).start()

    def take_b(src, d):
        pltpu.make_async_copy(src, weight.at[pl.ds(d * 32, 32), pl.ds(CUT, width - CUT)], sems.at[0]).start()

    start_pieces((a0, a1, a2, a3, a4), place, True, take_a)
    start_pieces((b0, b1, b2, b3, b4), place, False, take_b)

    def edge(r, _):
        slot = lax.rem(pages[r], slots)
        for k in range(3):
            edges[k, pl.ds(r, 1), :] = pool[k, pl.ds(slot, 1), :]
        return 0

    lax.fori_loop(0, count, edge, 0)
    pltpu.make_async_copy(weight, weight, sems.at[0]).wait()
    pltpu.make_async_copy(proj, proj, sems.at[1]).wait()
    pltpu.make_async_copy(dt_raw, dt_raw, sems.at[2]).wait()

    def project(n, _):
        at = pl.ds(pl.multiple_of(n * 256, 256), 256)
        total = jnp.zeros((tokens, 256), F32)
        for k in range(4):
            total = total + jnp.dot(
                normed[k], weight[pl.ds((m ^ k) * 512, 512), at], preferred_element_type=F32
            )
        xs[:, :, at] = total.astype(BF).astype(F32).reshape(drafts, count, 256)
        return 0

    lax.fori_loop(0, width // 256, project, 0)

    def mix(n, _):
        rows = pl.ds(pl.multiple_of((n // 4) * 16, 16), 16)
        at = pl.ds(pl.multiple_of((n % 4) * 256, 256), 256)
        acc = jnp.concatenate([accepted[rows, :]] * 2, axis=1)
        window = [edges[k, rows, at] for k in range(3)]
        kept = [window[0], window[0], window[0]]
        for p in range(1, 3):
            for k in range(3):
                kept[k] = jnp.where(acc + k == p, window[p], kept[k])
        tap = [taps[k : k + 1, at] for k in range(4)]
        base = bias[:, at]
        for t in range(drafts):
            now = xs[t, rows, at]
            mixed = base + tap[0] * window[0]
            mixed = mixed + tap[1] * window[1]
            mixed = mixed + tap[2] * window[2]
            mixed = mixed + tap[3] * now
            inputs_out[pl.ds(pl.multiple_of(t * count + (n // 4) * 16, 16), 16), at] = sigmoid_times(mixed).astype(BF)
            for k in range(3):
                kept[k] = jnp.where(acc + k == t + 3, now, kept[k])
            window = [window[1], window[2], now]
        for k in range(3):
            fresh[k, rows, at] = kept[k]
        return 0

    lax.fori_loop(0, (count // 16) * (width // 256), mix, 0)
    sums = lax.dot_general(
        proj[...], inputs_out[...], (((0,), (1,)), ((), ())), preferred_element_type=F32
    )
    sums_out[...] = sums[: sums_out.shape[0]]
    dt_wide[...] = dt_raw[...].astype(F32)
    for c in range(width // 128):
        dt_out[:, c * 128 : (c + 1) * 128] = dt_wide[pl.ds(c, 128, stride=8), :].astype(BF)
    pool_out[...] = pool[...]

    def settle(r, _):
        slot = lax.rem(pages[r], slots)
        for k in range(3):
            pool_out[k, pl.ds(slot, 1), :] = fresh[k, pl.ds(r, 1), :]
        return 0

    lax.fori_loop(0, count, settle, 0)


def scan_kernel(
    pages, accepted, sums_a, sums_b, dt, dt_bias, a_log, inputs, pool, ys_out, kept,
    low, both, delta, decay, start, wide, pick,
):
    tokens, width = inputs.shape
    count = accepted.shape[0]
    drafts = tokens // count
    states = a_log.shape[0]
    rank = low.shape[1]
    slots = pool.shape[0] // states

    def fetch(r, _):
        slot = lax.rem(pages[r], slots)
        for c in range(width // 128):
            start[c, pl.ds(pl.multiple_of(r * states, states), states), :] = pool[
                pl.ds(pl.multiple_of(slot * states, states), states), c * 128 : (c + 1) * 128
            ]
        return 0

    lax.fori_loop(0, count, fetch, 0)
    summed = sums_a[...] + sums_b[...].astype(F32)
    low[...] = summed[:rank].T.astype(BF)
    rest = summed[rank:]
    high = rest.astype(BF).astype(F32)
    middle = (rest - high).astype(BF).astype(F32)
    parts = [high, middle, rest - high - middle, jnp.zeros_like(rest)]
    both[...] = jnp.concatenate(parts, axis=0).T
    row = lax.broadcasted_iota(jnp.int32, (128, 128), 0)
    for q in range(2 * states):
        hit = ((row & (2 * states - 1)) == q) & (row < 6 * states)
        pick[:, q * 128 : (q + 1) * 128] = hit.astype(F32).astype(BF)

    def steps(n, _):
        at = pl.ds(pl.multiple_of(n * 256, 256), 256)
        value = jnp.dot(low[...], dt[:, at], preferred_element_type=F32) + dt_bias[:, at]
        delta[:, at] = jnp.maximum(value, 0.0) + jnp.log1p(jnp.exp(-jnp.abs(value)))
        return 0

    lax.fori_loop(0, width // 256, steps, 0)
    for s in range(states):
        decay[s] = jnp.broadcast_to(-jnp.exp(a_log[s : s + 1, :]) * LOG2E, (8, width))

    def some(rb, _):
        eight = pl.ds(pl.multiple_of(rb * 8, 8), 8)
        terms = jnp.concatenate(
            [both[pl.ds(pl.multiple_of(t * count + rb * 8, 8), 8), :] for t in range(drafts)], axis=0
        ).astype(BF)
        for q in range(0, 2 * states, 4):
            spread = jnp.dot(terms, pick[:, q * 128 : (q + 4) * 128], preferred_element_type=F32)
            for p in range(4):
                wide[:, q + p] = spread[:, p * 128 : (p + 1) * 128].reshape(drafts, 8, 128)
        last = accepted[eight, :] - 1

        def columns(cb, _):
            at = pl.ds(pl.multiple_of(cb * 128, 128), 128)
            first = tuple(
                start[cb, pl.ds(rb * 8 * states + s, 8, stride=states), :] for s in range(states)
            )

            def advance(t, state):
                rows = pl.ds(pl.multiple_of(t * count + rb * 8, 8), 8)
                d = delta[rows, at]
                drive = d * inputs[rows, at].astype(F32)
                here = last == t
                out = None
                nexts = []
                for s in range(states):
                    new = jnp.exp2(d * decay[s, :, at]) * state[s] + drive * wide[t, s]
                    term = new * wide[t, states + s]
                    out = term if out is None else out + term
                    pltpu.store(kept.at[cb, pl.ds(pl.multiple_of(s * count + rb * 8, 8), 8), :], new, mask=here)
                    nexts.append(new)
                ys_out[rows, at] = out
                return tuple(nexts)

            lax.fori_loop(0, drafts, advance, first, unroll=4)
            return 0

        lax.fori_loop(0, width // 128, columns, 0)
        return 0

    lax.fori_loop(0, count // 8, some, 0)


def settle_kernel(pages, kept, pool, pool_out):
    chunks, rows, _ = kept.shape
    count = pages.shape[0]
    states = rows // count
    slots = pool.shape[0] // states

    def carry_over(n, _):
        at = pl.ds(pl.multiple_of(n * states, states), states)
        pool_out[at, :] = pool[at, :]
        return 0

    lax.fori_loop(0, slots, carry_over, 0)

    def settle(r, _):
        slot = lax.rem(pages[r], slots)
        for c in range(chunks):
            for s in range(0, states, 8):
                pool_out[
                    pl.ds(pl.multiple_of(slot * states + s, 8), 8), c * 128 : (c + 1) * 128
                ] = kept[c, pl.ds(s * count + r, 8, stride=count), :]
        return 0

    lax.fori_loop(0, count, settle, 0)


def gate_kernel(
    where, normed, inputs, ys, skip, second, send_out, keep_out, weight, outer, gated, sems
):
    m = where[1]
    tokens, width = gated.shape
    for z in range(SIDE):
        pltpu.make_async_copy(second.at[z, :, pl.ds(0, 32), :], weight.at[z], sems.at[0]).start()
    for z in range(SIDE):
        pltpu.make_async_copy(second.at[z, :, pl.ds(32, 32), :], outer.at[z], sems.at[1]).start()
    pltpu.make_async_copy(weight, weight, sems.at[0]).wait()

    def gate(n, _):
        at = pl.ds(pl.multiple_of(n * 256, 256), 256)
        total = jnp.zeros((tokens, 256), F32)
        for k in range(4):
            block = weight[m ^ k, :, :, at].reshape(512, 256)
            total = total + jnp.dot(normed[k], block, preferred_element_type=F32)
        gates = total.astype(BF).astype(F32)
        mixed = ys[:, at] + skip[:, at] * inputs[:, at].astype(F32)
        gated[:, at] = (mixed * sigmoid_times(gates)).astype(BF)
        return 0

    lax.fori_loop(0, width // 256, gate, 0)
    pltpu.make_async_copy(outer, outer, sems.at[1]).wait()

    def out(part, _):
        column = pl.ds(pl.multiple_of((part & 1) * 256, 256), 256)
        for core in range(2):
            block = m ^ ((part & 2) + core)
            rows = outer[block, pl.ds((part & 1) * 8, 8), :, :].reshape(256, width)
            value = lax.dot_general(
                gated[...], rows, (((1,), (1,)), ((), ())), preferred_element_type=F32
            )
            if core:
                send_out[part >> 1, :, column] = value.astype(BF)
            else:
                keep_out[part >> 1, :, column] = value
        return 0

    lax.fori_loop(0, 4, out, 0)


def join_kernel(targets, keep, near, far, hidden, out, total):
    tokens, width = hidden.shape
    count = targets.shape[0]
    drafts = tokens // count
    order = order_matrix(tokens, tokens, drafts, count)
    base = jnp.dot(order, hidden[...], preferred_element_type=F32)
    summed = keep[0] + near[0].astype(F32) + far[...].astype(F32)
    rounded = (summed + base).astype(BF)
    back = lax.dot_general(order, rounded, (((0,), (0,)), ((), ())), preferred_element_type=F32)
    total[...] = back.astype(BF).reshape(count, drafts, width)
    out[...] = jnp.zeros(out.shape, BF)

    def place(r, _):
        out[lax.div(targets[r], count)] = total[r]
        return 0

    lax.fori_loop(0, count, place, 0)


def unpack_kernel(where, targets, got, out):
    count = targets.shape[0]
    peers = got.shape[0]

    def take(r, _):
        source = lax.rem(2 * where[0] - lax.div(targets[r], count) + 2 * peers, peers)
        out[r] = got[source]
        return 0

    lax.fori_loop(0, count, take, 0)


def params():
    return pltpu.CompilerParams(vmem_limit_bytes=56 << 20)


def on_device(
    hidden, norm_gain, in_x, in_z, conv_weight, conv_bias, x_proj, dt_proj, dt_bias, a_log, skip,
    out_proj, state_pool, conv_pool, permutation, page_table, accepted,
):
    count, drafts, part = hidden.shape
    tokens = count * drafts
    width = in_x.shape[1]
    slots, states, _ = state_pool.shape
    rank = x_proj.shape[1] - 2 * states
    where = jnp.stack([lax.axis_index("dp"), lax.axis_index("mp")]).astype(jnp.int32)
    peers = lax.axis_size("dp")

    extra = jnp.concatenate(
        [
            x_proj,
            jnp.zeros((16, 256 - x_proj.shape[1]), BF),
            dt_proj.reshape(16, 128),
            jnp.zeros((16, width - CUT), BF),
        ],
        axis=1,
    )
    first = direct(jnp.concatenate([in_x, extra], axis=0), 0)
    middle_a = direct(first[:, :, :CUT], 2)
    middle_b = direct(first[:, :32, CUT:], 1)
    middle_a, middle_b = lax.optimization_barrier((middle_a, middle_b))
    sides_a, sides_b = ring_one(middle_a, 1), ring_one(middle_b, 2)
    first_a = ring_two(middle_a, 1, sides_a)
    first_b = ring_two(middle_b, 2, sides_b)

    flat = hidden.reshape(tokens, part)
    sent = jnp.concatenate([flat, jnp.broadcast_to(norm_gain[None], (16, part))], axis=0)
    sent = after(sent, middle_a, middle_b)
    near = across(sent, 1)
    far = across(sent, 2)
    both = across(far, 1)
    normed = pl.pallas_call(
        prep_kernel,
        out_shape=jax.ShapeDtypeStruct((4, tokens, part), BF),
        in_specs=[VMEM] * 4,
        out_specs=VMEM,
        scratch_shapes=[pltpu.VMEM((4, tokens, part), BF)],
        compiler_params=params(),
        cost_estimate=pl.CostEstimate(flops=1_000_000, bytes_accessed=1 << 10, transcendentals=0),
        name="prep",
    )(sent, *after((near, far, both), sides_a, sides_b))

    pair = jnp.concatenate([in_z, out_proj.T], axis=0)
    second = lax.all_gather(pair, "dp", axis=0).reshape(SIDE, 16, 64, width)

    wide_accepted = jnp.broadcast_to(accepted[:, None], (count, 128))
    inputs, sums, dt, new_conv = pl.pallas_call(
        front_kernel,
        out_shape=(
            jax.ShapeDtypeStruct((tokens, width), BF),
            jax.ShapeDtypeStruct((rank + 2 * states, tokens), F32),
            jax.ShapeDtypeStruct((rank, width), BF),
            jax.ShapeDtypeStruct((3, slots, width), F32),
        ),
        in_specs=[SMEM, SMEM] + [VMEM] * 2 + [ANY] * 10 + [VMEM] * 3,
        out_specs=(VMEM,) * 4,
        scratch_shapes=[
            pltpu.VMEM((2048, width), BF),
            pltpu.VMEM((1024, 256), BF),
            pltpu.VMEM((1024, 128), BF),
            pltpu.VMEM((1024, 128), F32),
            pltpu.VMEM((drafts, count, width), F32),
            pltpu.VMEM((3, count, width), F32),
            pltpu.VMEM((3, count, width), F32),
            pltpu.SemaphoreType.DMA((3,)),
        ],
        compiler_params=params(),
        cost_estimate=pl.CostEstimate(flops=12_000_000_000, bytes_accessed=1 << 10, transcendentals=0),
        name="front",
    )(
        where, page_table, wide_accepted, normed, *first_a, *first_b,
        conv_weight, conv_bias[None], conv_pool.transpose(1, 0, 2),
    )

    sums = sums + across(sums, 1)
    other = across(sums.astype(BF), 2)
    ys, kept = pl.pallas_call(
        scan_kernel,
        out_shape=(
            jax.ShapeDtypeStruct((tokens, width), F32),
            jax.ShapeDtypeStruct((width // 128, states * count, 128), F32),
        ),
        in_specs=[SMEM] + [VMEM] * 8,
        out_specs=(VMEM,) * 2,
        scratch_shapes=[
            pltpu.VMEM((tokens, rank), BF),
            pltpu.VMEM((tokens, 128), F32),
            pltpu.VMEM((tokens, width), F32),
            pltpu.VMEM((states, 8, width), F32),
            pltpu.VMEM((width // 128, count * states, 128), F32),
            pltpu.VMEM((drafts, 2 * states, 8, 128), F32),
            pltpu.VMEM((128, 2 * states * 128), BF),
        ],
        compiler_params=params(),
        cost_estimate=pl.CostEstimate(flops=1_000_000, bytes_accessed=1 << 10, transcendentals=0),
        name="scan",
    )(
        page_table, wide_accepted, sums, other, dt, dt_bias[None], a_log, inputs,
        state_pool.reshape(slots * states, width),
    )

    new_state = pl.pallas_call(
        settle_kernel,
        out_shape=jax.ShapeDtypeStruct((slots * states, width), F32),
        in_specs=[SMEM, VMEM, VMEM],
        out_specs=VMEM,
        compiler_params=params(),
        cost_estimate=pl.CostEstimate(flops=1_000_000, bytes_accessed=1 << 10, transcendentals=0),
        name="settle",
    )(page_table, kept, state_pool.reshape(slots * states, width))

    send, keep = pl.pallas_call(
        gate_kernel,
        out_shape=(
            jax.ShapeDtypeStruct((2, tokens, part), BF),
            jax.ShapeDtypeStruct((2, tokens, part), F32),
        ),
        in_specs=[SMEM] + [VMEM] * 4 + [ANY],
        out_specs=(VMEM,) * 2,
        scratch_shapes=[
            pltpu.VMEM((SIDE, 16, 32, width), BF),
            pltpu.VMEM((SIDE, 16, 32, width), BF),
            pltpu.VMEM((tokens, width), BF),
            pltpu.SemaphoreType.DMA((2,)),
        ],
        compiler_params=params(),
        cost_estimate=pl.CostEstimate(flops=1_000_000, bytes_accessed=1 << 10, transcendentals=0),
        name="gate",
    )(where, normed, inputs, ys, skip[None], second)
    got = across(send, 1)
    remote = across((keep[1] + got[1].astype(F32)).astype(BF), 2)
    packed = pl.pallas_call(
        join_kernel,
        out_shape=jax.ShapeDtypeStruct((peers, drafts, part), BF),
        in_specs=[SMEM] + [VMEM] * 4,
        out_specs=VMEM,
        scratch_shapes=[pltpu.VMEM((count, drafts, part), BF)],
        compiler_params=params(),
        cost_estimate=pl.CostEstimate(flops=1_000_000, bytes_accessed=1 << 10, transcendentals=0),
        name="join",
    )(permutation, keep, got, remote, flat)
    arrived = lax.all_to_all(packed, "dp", split_axis=0, concat_axis=0, tiled=True)
    verified = pl.pallas_call(
        unpack_kernel,
        out_shape=jax.ShapeDtypeStruct((count, drafts, part), BF),
        in_specs=[SMEM, SMEM, VMEM],
        out_specs=VMEM,
        name="unpack",
    )(where, permutation, arrived)
    return (
        verified,
        new_state.reshape(slots, states, width),
        new_conv.transpose(1, 0, 2),
    )


def solution(mesh):
    return jax.shard_map(
        on_device,
        mesh=mesh,
        in_specs=(
            P("dp", None, "mp"),
            P("mp"),
            P("dp", "mp"),
            P("dp", "mp"),
            P(None, "mp"),
            P("mp"),
            P(("mp", "dp"), None),
            P("dp", "mp"),
            P("mp"),
            P(None, "mp"),
            P("mp"),
            P("mp", "dp"),
            P("dp", None, "mp"),
            P("dp", None, "mp"),
            P("dp"),
            P("dp"),
            P("dp"),
        ),
        out_specs=(P("dp", None, "mp"), P("dp", None, "mp"), P("dp", None, "mp")),
        check_vma=False,
    )
```

```python
import jax
import jax.numpy as jnp
from jax import lax
from jax.experimental import pallas as pl
from jax.experimental.pallas import tpu as pltpu
from jax.sharding import PartitionSpec as P

EPS = 1e-05
LOG2E = 1.4426950408889634
BF = jnp.bfloat16
F32 = jnp.float32
SIDE = 4
CUT = 384

VMEM = pl.BlockSpec(memory_space=pltpu.VMEM)
SMEM = pl.BlockSpec(memory_space=pltpu.SMEM)
ANY = pl.BlockSpec(memory_space=pl.ANY)


def shift_pairs(axis, step):
    pairs = []
    for z in range(SIDE):
        for y in range(SIDE):
            for x in range(SIDE):
                to = [z, y, x]
                to[axis] = (to[axis] + step) % SIDE
                pairs.append(((z * SIDE + y) * SIDE + x, (to[0] * SIDE + to[1]) * SIDE + to[2]))
    return pairs


def hop(value, axis, step):
    return lax.ppermute(value, "dp", shift_pairs(axis, step))


def across(value, flip):
    return lax.ppermute(value, "mp", [(m, m ^ flip) for m in range(4)])


def after(value, *others):
    return lax.optimization_barrier((value, others))[0]


def ring_one(block, axis):
    return hop(block, axis, -1), hop(block, axis, 1)


def ring_two(block, axis, sides):
    half = block.shape[0] // 2
    above, below = sides
    return block, above, hop(below[:half], axis, 1), hop(above[half:], axis, -1), below


def send_direct(block, axis):
    return block, hop(block, axis, -1), hop(block, axis, 2), hop(block, axis, 1)


def direct(block, axis):
    return jnp.stack(send_direct(block, axis))


def start_pieces(pieces, place, middle_first, body):
    z, y, x = place
    own, above, low, high, below = pieces

    def one(n, _):
        i, k = n >> 2, n & 3
        dz = (z + k) & 3

        def piece(f, ref, at):
            if middle_first:
                dx, dy = (x + i) & 3, (y + f) & 3
            else:
                dy, dx = (y + i) & 3, (x + f) & 3
            body(ref.at[at, k], (dz * SIDE + dy) * SIDE + dx)

        piece(0, own, i)
        piece(1, above, i)
        piece(3, below, i)

        @pl.when(i < 2)
        def _():
            piece(2, low, i)

        @pl.when(i >= 2)
        def _():
            piece(2, high, i - 2)

        return 0

    lax.fori_loop(0, SIDE * SIDE, one, 0)


def place_of(where):
    d = where[0]
    return d >> 4, (d >> 2) & 3, d & 3


def sigmoid_times(value):
    return value / (1.0 + jnp.exp(-value))


def order_matrix(rows, columns, drafts, count):
    i = lax.broadcasted_iota(jnp.int32, (rows, columns), 0)
    j = lax.broadcasted_iota(jnp.int32, (rows, columns), 1)
    return ((i % count) * drafts + i // count == j).astype(BF)


def prep_kernel(h0, h1, h2, h3, normed_out, plain):
    tokens = normed_out.shape[1]
    count = 32
    blocks = (h0, h1, h2, h3)
    step = 32

    def norm(n, _):
        at = pl.ds(pl.multiple_of(n * step, step), step)
        rows = [h[at, :].astype(F32) for h in blocks]
        total = sum(jnp.sum(r * r, axis=1, keepdims=True) for r in rows)
        scale = lax.rsqrt(total / (4.0 * rows[0].shape[1]) + EPS)
        for k, h in enumerate(blocks):
            gain = h[pl.ds(tokens, 1), :].astype(F32)
            plain[k, at, :] = (rows[k] * scale * gain).astype(BF)
        return 0

    lax.fori_loop(0, tokens // step, norm, 0)
    order = order_matrix(tokens, tokens, tokens // count, count)
    for k in range(4):
        normed_out[k] = jnp.dot(order, plain[k], preferred_element_type=F32).astype(BF)


def front_kernel(
    where, pages, accepted, normed, a0, a1, a2, a3, a4, b0, b1, b2, b3, b4,
    taps, bias, pool, inputs_out, sums_out, dt_out, pool_out,
    weight, proj, dt_raw, dt_wide, xs, edges, fresh, sems,
):
    place = place_of(where)
    m = where[1]
    drafts, count, width = xs.shape
    tokens = drafts * count
    slots = pool.shape[1]

    def take_a(src, d):
        pltpu.make_async_copy(src.at[pl.ds(0, 32), :], weight.at[pl.ds(d * 32, 32), pl.ds(0, CUT)], sems.at[0]).start()
        pltpu.make_async_copy(src.at[pl.ds(32, 16), pl.ds(0, 256)], proj.at[pl.ds(d * 16, 16), :], sems.at[1]).start()
        pltpu.make_async_copy(src.at[pl.ds(32, 16), pl.ds(256, 128)], dt_raw.at[pl.ds(d * 16, 16), :], sems.at[2]).start()

    def take_b(src, d):
        pltpu.make_async_copy(src, weight.at[pl.ds(d * 32, 32), pl.ds(CUT, width - CUT)], sems.at[0]).start()

    start_pieces((a0, a1, a2, a3, a4), place, True, take_a)
    start_pieces((b0, b1, b2, b3, b4), place, False, take_b)

    def edge(r, _):
        slot = lax.rem(pages[r], slots)
        for k in range(3):
            edges[k, pl.ds(r, 1), :] = pool[k, pl.ds(slot, 1), :]
        return 0

    lax.fori_loop(0, count, edge, 0)
    pltpu.make_async_copy(weight, weight, sems.at[0]).wait()
    pltpu.make_async_copy(proj, proj, sems.at[1]).wait()
    pltpu.make_async_copy(dt_raw, dt_raw, sems.at[2]).wait()

    def project(n, _):
        at = pl.ds(pl.multiple_of(n * 256, 256), 256)
        total = jnp.zeros((tokens, 256), F32)
        for k in range(4):
            total = total + jnp.dot(
                normed[k], weight[pl.ds((m ^ k) * 512, 512), at], preferred_element_type=F32
            )
        xs[:, :, at] = total.astype(BF).astype(F32).reshape(drafts, count, 256)
        return 0

    lax.fori_loop(0, width // 256, project, 0)

    def mix(n, _):
        rows = pl.ds(pl.multiple_of((n // 4) * 16, 16), 16)
        at = pl.ds(pl.multiple_of((n % 4) * 256, 256), 256)
        acc = jnp.concatenate([accepted[rows, :]] * 2, axis=1)
        window = [edges[k, rows, at] for k in range(3)]
        kept = [window[0], window[0], window[0]]
        for p in range(1, 3):
            for k in range(3):
                kept[k] = jnp.where(acc + k == p, window[p], kept[k])
        tap = [taps[k : k + 1, at] for k in range(4)]
        base = bias[:, at]
        for t in range(drafts):
            now = xs[t, rows, at]
            mixed = base + tap[0] * window[0]
            mixed = mixed + tap[1] * window[1]
            mixed = mixed + tap[2] * window[2]
            mixed = mixed + tap[3] * now
            inputs_out[pl.ds(pl.multiple_of(t * count + (n // 4) * 16, 16), 16), at] = sigmoid_times(mixed).astype(BF)
            for k in range(3):
                kept[k] = jnp.where(acc + k == t + 3, now, kept[k])
            window = [window[1], window[2], now]
        for k in range(3):
            fresh[k, rows, at] = kept[k]
        return 0

    lax.fori_loop(0, (count // 16) * (width // 256), mix, 0)
    sums = lax.dot_general(
        proj[...], inputs_out[...], (((0,), (1,)), ((), ())), preferred_element_type=F32
    )
    sums_out[...] = sums[: sums_out.shape[0]]
    dt_wide[...] = dt_raw[...].astype(F32)
    for c in range(width // 128):
        dt_out[:, c * 128 : (c + 1) * 128] = dt_wide[pl.ds(c, 128, stride=8), :].astype(BF)
    pool_out[...] = pool[...]

    def settle(r, _):
        slot = lax.rem(pages[r], slots)
        for k in range(3):
            pool_out[k, pl.ds(slot, 1), :] = fresh[k, pl.ds(r, 1), :]
        return 0

    lax.fori_loop(0, count, settle, 0)


def scan_kernel(
    pages, accepted, sums_a, sums_b, dt, dt_bias, a_log, inputs, pool, ys_out, kept,
    low, both, delta, decay, start, wide, pick,
):
    tokens, width = inputs.shape
    count = accepted.shape[0]
    drafts = tokens // count
    states = a_log.shape[0]
    rank = low.shape[1]
    slots = pool.shape[0] // states

    def fetch(r, _):
        slot = lax.rem(pages[r], slots)
        for c in range(width // 128):
            start[c, pl.ds(pl.multiple_of(r * states, states), states), :] = pool[
                pl.ds(pl.multiple_of(slot * states, states), states), c * 128 : (c + 1) * 128
            ]
        return 0

    lax.fori_loop(0, count, fetch, 0)
    summed = sums_a[...] + sums_b[...].astype(F32)
    low[...] = summed[:rank].T.astype(BF)
    rest = summed[rank:]
    high = rest.astype(BF).astype(F32)
    middle = (rest - high).astype(BF).astype(F32)
    parts = [high, middle, rest - high - middle, jnp.zeros_like(rest)]
    both[...] = jnp.concatenate(parts, axis=0).T
    row = lax.broadcasted_iota(jnp.int32, (128, 128), 0)
    for q in range(2 * states):
        hit = ((row & (2 * states - 1)) == q) & (row < 6 * states)
        pick[:, q * 128 : (q + 1) * 128] = hit.astype(F32).astype(BF)

    def steps(n, _):
        at = pl.ds(pl.multiple_of(n * 256, 256), 256)
        value = jnp.dot(low[...], dt[:, at], preferred_element_type=F32) + dt_bias[:, at]
        delta[:, at] = jnp.maximum(value, 0.0) + jnp.log1p(jnp.exp(-jnp.abs(value)))
        return 0

    lax.fori_loop(0, width // 256, steps, 0)
    for s in range(states):
        decay[s] = jnp.broadcast_to(-jnp.exp(a_log[s : s + 1, :]) * LOG2E, (8, width))

    def some(rb, _):
        eight = pl.ds(pl.multiple_of(rb * 8, 8), 8)
        terms = jnp.concatenate(
            [both[pl.ds(pl.multiple_of(t * count + rb * 8, 8), 8), :] for t in range(drafts)], axis=0
        ).astype(BF)
        for q in range(0, 2 * states, 4):
            spread = jnp.dot(terms, pick[:, q * 128 : (q + 4) * 128], preferred_element_type=F32)
            for p in range(4):
                wide[:, q + p] = spread[:, p * 128 : (p + 1) * 128].reshape(drafts, 8, 128)
        last = accepted[eight, :] - 1

        def columns(cb, _):
            at = pl.ds(pl.multiple_of(cb * 128, 128), 128)
            first = tuple(
                start[cb, pl.ds(rb * 8 * states + s, 8, stride=states), :] for s in range(states)
            )

            def advance(t, state):
                rows = pl.ds(pl.multiple_of(t * count + rb * 8, 8), 8)
                d = delta[rows, at]
                drive = d * inputs[rows, at].astype(F32)
                here = last == t
                out = None
                nexts = []
                for s in range(states):
                    new = jnp.exp2(d * decay[s, :, at]) * state[s] + drive * wide[t, s]
                    term = new * wide[t, states + s]
                    out = term if out is None else out + term
                    pltpu.store(kept.at[cb, pl.ds(pl.multiple_of(s * count + rb * 8, 8), 8), :], new, mask=here)
                    nexts.append(new)
                ys_out[rows, at] = out
                return tuple(nexts)

            lax.fori_loop(0, drafts, advance, first, unroll=4)
            return 0

        lax.fori_loop(0, width // 128, columns, 0)
        return 0

    lax.fori_loop(0, count // 8, some, 0)


def settle_kernel(pages, kept, pool, pool_out):
    chunks, rows, _ = kept.shape
    count = pages.shape[0]
    states = rows // count
    slots = pool.shape[0] // states

    def carry_over(n, _):
        at = pl.ds(pl.multiple_of(n * states, states), states)
        pool_out[at, :] = pool[at, :]
        return 0

    lax.fori_loop(0, slots, carry_over, 0)

    def settle(r, _):
        slot = lax.rem(pages[r], slots)
        for c in range(chunks):
            for s in range(0, states, 8):
                pool_out[
                    pl.ds(pl.multiple_of(slot * states + s, 8), 8), c * 128 : (c + 1) * 128
                ] = kept[c, pl.ds(s * count + r, 8, stride=count), :]
        return 0

    lax.fori_loop(0, count, settle, 0)


def gate_kernel(
    where, normed, inputs, ys, skip, second, send_out, keep_out, weight, outer, gated, sems
):
    m = where[1]
    tokens, width = gated.shape
    for z in range(SIDE):
        at = (z + SIDE - (where[0] >> 4)) & 3
        pltpu.make_async_copy(second.at[:, at, pl.ds(0, 32), :], weight.at[z], sems.at[0]).start()
    for z in range(SIDE):
        at = (z + SIDE - (where[0] >> 4)) & 3
        pltpu.make_async_copy(second.at[:, at, pl.ds(32, 32), :], outer.at[z], sems.at[1]).start()
    pltpu.make_async_copy(weight, weight, sems.at[0]).wait()

    def gate(n, _):
        at = pl.ds(pl.multiple_of(n * 256, 256), 256)
        total = jnp.zeros((tokens, 256), F32)
        for k in range(4):
            block = weight[m ^ k, :, :, at].reshape(512, 256)
            total = total + jnp.dot(normed[k], block, preferred_element_type=F32)
        gates = total.astype(BF).astype(F32)
        mixed = ys[:, at] + skip[:, at] * inputs[:, at].astype(F32)
        gated[:, at] = (mixed * sigmoid_times(gates)).astype(BF)
        return 0

    lax.fori_loop(0, width // 256, gate, 0)
    pltpu.make_async_copy(outer, outer, sems.at[1]).wait()

    def out(part, _):
        column = pl.ds(pl.multiple_of((part & 1) * 256, 256), 256)
        for core in range(2):
            block = m ^ ((part & 2) + core)
            rows = outer[block, pl.ds((part & 1) * 8, 8), :, :].reshape(256, width)
            value = lax.dot_general(
                gated[...], rows, (((1,), (1,)), ((), ())), preferred_element_type=F32
            )
            if core:
                send_out[part >> 1, :, column] = value.astype(BF)
            else:
                keep_out[part >> 1, :, column] = value
        return 0

    lax.fori_loop(0, 4, out, 0)


def join_kernel(targets, keep, near, far, hidden, out, total):
    tokens, width = hidden.shape
    count = targets.shape[0]
    drafts = tokens // count
    order = order_matrix(tokens, tokens, drafts, count)
    base = jnp.dot(order, hidden[...], preferred_element_type=F32)
    summed = keep[0] + near[0].astype(F32) + far[...].astype(F32)
    rounded = (summed + base).astype(BF)
    back = lax.dot_general(order, rounded, (((0,), (0,)), ((), ())), preferred_element_type=F32)
    total[...] = back.astype(BF).reshape(count, drafts, width)
    out[...] = jnp.zeros(out.shape, BF)

    def place(r, _):
        out[lax.div(targets[r], count)] = total[r]
        return 0

    lax.fori_loop(0, count, place, 0)


def unpack_kernel(where, targets, got, out):
    count = targets.shape[0]
    peers = got.shape[0]

    def take(r, _):
        source = lax.rem(2 * where[0] - lax.div(targets[r], count) + 2 * peers, peers)
        out[r] = got[source]
        return 0

    lax.fori_loop(0, count, take, 0)


def params():
    return pltpu.CompilerParams(vmem_limit_bytes=56 << 20)


def on_device(
    hidden, norm_gain, in_x, in_z, conv_weight, conv_bias, x_proj, dt_proj, dt_bias, a_log, skip,
    out_proj, state_pool, conv_pool, permutation, page_table, accepted,
):
    count, drafts, part = hidden.shape
    tokens = count * drafts
    width = in_x.shape[1]
    slots, states, _ = state_pool.shape
    rank = x_proj.shape[1] - 2 * states
    where = jnp.stack([lax.axis_index("dp"), lax.axis_index("mp")]).astype(jnp.int32)
    peers = lax.axis_size("dp")

    extra = jnp.concatenate(
        [
            x_proj,
            jnp.zeros((16, 256 - x_proj.shape[1]), BF),
            dt_proj.reshape(16, 128),
            jnp.zeros((16, width - CUT), BF),
        ],
        axis=1,
    )
    first = direct(jnp.concatenate([in_x, extra], axis=0), 0)
    middle_a = direct(first[:, :, :CUT], 2)
    middle_b = direct(first[:, :32, CUT:], 1)
    middle_a, middle_b = lax.optimization_barrier((middle_a, middle_b))
    sides_a, sides_b = ring_one(middle_a, 1), ring_one(middle_b, 2)
    first_a = ring_two(middle_a, 1, sides_a)
    first_b = ring_two(middle_b, 2, sides_b)

    flat = hidden.reshape(tokens, part)
    sent = jnp.concatenate([flat, jnp.broadcast_to(norm_gain[None], (16, part))], axis=0)
    sent = after(sent, middle_a, middle_b)
    near = across(sent, 1)
    far = across(sent, 2)
    both = across(far, 1)
    normed = pl.pallas_call(
        prep_kernel,
        out_shape=jax.ShapeDtypeStruct((4, tokens, part), BF),
        in_specs=[VMEM] * 4,
        out_specs=VMEM,
        scratch_shapes=[pltpu.VMEM((4, tokens, part), BF)],
        compiler_params=params(),
        cost_estimate=pl.CostEstimate(flops=1_000_000, bytes_accessed=1 << 10, transcendentals=0),
        name="prep",
    )(sent, *after((near, far, both), sides_a, sides_b))

    pair = after(jnp.concatenate([in_z, out_proj.T], axis=0), first)
    second = lax.all_gather(
        jnp.stack(after(send_direct(pair, 0), middle_a, middle_b)), "dp", axis=0,
        axis_index_groups=[[z * 16 + i for i in range(16)] for z in range(SIDE)],
    )

    wide_accepted = jnp.broadcast_to(accepted[:, None], (count, 128))
    inputs, sums, dt, new_conv = pl.pallas_call(
        front_kernel,
        out_shape=(
            jax.ShapeDtypeStruct((tokens, width), BF),
            jax.ShapeDtypeStruct((rank + 2 * states, tokens), F32),
            jax.ShapeDtypeStruct((rank, width), BF),
            jax.ShapeDtypeStruct((3, slots, width), F32),
        ),
        in_specs=[SMEM, SMEM] + [VMEM] * 2 + [ANY] * 10 + [VMEM] * 3,
        out_specs=(VMEM,) * 4,
        scratch_shapes=[
            pltpu.VMEM((2048, width), BF),
            pltpu.VMEM((1024, 256), BF),
            pltpu.VMEM((1024, 128), BF),
            pltpu.VMEM((1024, 128), F32),
            pltpu.VMEM((drafts, count, width), F32),
            pltpu.VMEM((3, count, width), F32),
            pltpu.VMEM((3, count, width), F32),
            pltpu.SemaphoreType.DMA((3,)),
        ],
        compiler_params=params(),
        cost_estimate=pl.CostEstimate(flops=12_000_000_000, bytes_accessed=1 << 10, transcendentals=0),
        name="front",
    )(
        where, page_table, wide_accepted, normed, *first_a, *first_b,
        conv_weight, conv_bias[None], conv_pool.transpose(1, 0, 2),
    )

    sums = sums + across(sums, 1)
    other = across(sums.astype(BF), 2)
    ys, kept = pl.pallas_call(
        scan_kernel,
        out_shape=(
            jax.ShapeDtypeStruct((tokens, width), F32),
            jax.ShapeDtypeStruct((width // 128, states * count, 128), F32),
        ),
        in_specs=[SMEM] + [VMEM] * 8,
        out_specs=(VMEM,) * 2,
        scratch_shapes=[
            pltpu.VMEM((tokens, rank), BF),
            pltpu.VMEM((tokens, 128), F32),
            pltpu.VMEM((tokens, width), F32),
            pltpu.VMEM((states, 8, width), F32),
            pltpu.VMEM((width // 128, count * states, 128), F32),
            pltpu.VMEM((drafts, 2 * states, 8, 128), F32),
            pltpu.VMEM((128, 2 * states * 128), BF),
        ],
        compiler_params=params(),
        cost_estimate=pl.CostEstimate(flops=1_000_000, bytes_accessed=1 << 10, transcendentals=0),
        name="scan",
    )(
        page_table, wide_accepted, sums, other, dt, dt_bias[None], a_log, inputs,
        state_pool.reshape(slots * states, width),
    )

    new_state = pl.pallas_call(
        settle_kernel,
        out_shape=jax.ShapeDtypeStruct((slots * states, width), F32),
        in_specs=[SMEM, VMEM, VMEM],
        out_specs=VMEM,
        compiler_params=params(),
        cost_estimate=pl.CostEstimate(flops=1_000_000, bytes_accessed=1 << 10, transcendentals=0),
        name="settle",
    )(page_table, kept, state_pool.reshape(slots * states, width))

    send, keep = pl.pallas_call(
        gate_kernel,
        out_shape=(
            jax.ShapeDtypeStruct((2, tokens, part), BF),
            jax.ShapeDtypeStruct((2, tokens, part), F32),
        ),
        in_specs=[SMEM] + [VMEM] * 4 + [ANY],
        out_specs=(VMEM,) * 2,
        scratch_shapes=[
            pltpu.VMEM((SIDE, 16, 32, width), BF),
            pltpu.VMEM((SIDE, 16, 32, width), BF),
            pltpu.VMEM((tokens, width), BF),
            pltpu.SemaphoreType.DMA((2,)),
        ],
        compiler_params=params(),
        cost_estimate=pl.CostEstimate(flops=1_000_000, bytes_accessed=1 << 10, transcendentals=0),
        name="gate",
    )(where, normed, inputs, ys, skip[None], second)
    got = across(send, 1)
    remote = across((keep[1] + got[1].astype(F32)).astype(BF), 2)
    packed = pl.pallas_call(
        join_kernel,
        out_shape=jax.ShapeDtypeStruct((peers, drafts, part), BF),
        in_specs=[SMEM] + [VMEM] * 4,
        out_specs=VMEM,
        scratch_shapes=[pltpu.VMEM((count, drafts, part), BF)],
        compiler_params=params(),
        cost_estimate=pl.CostEstimate(flops=1_000_000, bytes_accessed=1 << 10, transcendentals=0),
        name="join",
    )(permutation, keep, got, remote, flat)
    arrived = lax.all_to_all(packed, "dp", split_axis=0, concat_axis=0, tiled=True)
    verified = pl.pallas_call(
        unpack_kernel,
        out_shape=jax.ShapeDtypeStruct((count, drafts, part), BF),
        in_specs=[SMEM, SMEM, VMEM],
        out_specs=VMEM,
        name="unpack",
    )(where, permutation, arrived)
    return (
        verified,
        new_state.reshape(slots, states, width),
        new_conv.transpose(1, 0, 2),
    )


def solution(mesh):
    return jax.shard_map(
        on_device,
        mesh=mesh,
        in_specs=(
            P("dp", None, "mp"),
            P("mp"),
            P("dp", "mp"),
            P("dp", "mp"),
            P(None, "mp"),
            P("mp"),
            P(("mp", "dp"), None),
            P("dp", "mp"),
            P("mp"),
            P(None, "mp"),
            P("mp"),
            P("mp", "dp"),
            P("dp", None, "mp"),
            P("dp", None, "mp"),
            P("dp"),
            P("dp"),
            P("dp"),
        ),
        out_specs=(P("dp", None, "mp"), P("dp", None, "mp"), P("dp", None, "mp")),
        check_vma=False,
    )
```

```python
import jax
import jax.numpy as jnp
from jax import lax
from jax.experimental import pallas as pl
from jax.experimental.pallas import tpu as pltpu
from jax.sharding import PartitionSpec as P

EPS = 1e-05
LOG2E = 1.4426950408889634
BF = jnp.bfloat16
F32 = jnp.float32
SIDE = 4
CUT = 384

VMEM = pl.BlockSpec(memory_space=pltpu.VMEM)
SMEM = pl.BlockSpec(memory_space=pltpu.SMEM)
ANY = pl.BlockSpec(memory_space=pl.ANY)


def shift_pairs(axis, step):
    pairs = []
    for z in range(SIDE):
        for y in range(SIDE):
            for x in range(SIDE):
                to = [z, y, x]
                to[axis] = (to[axis] + step) % SIDE
                pairs.append(((z * SIDE + y) * SIDE + x, (to[0] * SIDE + to[1]) * SIDE + to[2]))
    return pairs


def hop(value, axis, step):
    return lax.ppermute(value, "dp", shift_pairs(axis, step))


def across(value, flip):
    return lax.ppermute(value, "mp", [(m, m ^ flip) for m in range(4)])


def after(value, *others):
    return lax.optimization_barrier((value, others))[0]


def ring_one(block, axis):
    return hop(block, axis, -1), hop(block, axis, 1)


def ring_two(block, axis, sides):
    half = block.shape[0] // 2
    above, below = sides
    return block, above, hop(below[:half], axis, 1), hop(above[half:], axis, -1), below


def send_direct(block, axis):
    return block, hop(block, axis, -1), hop(block, axis, 2), hop(block, axis, 1)


def direct(block, axis):
    return jnp.stack(send_direct(block, axis))


def start_pieces(pieces, place, middle_first, body):
    z, y, x = place
    own, above, low, high, below = pieces

    def one(n, _):
        i, k = n >> 2, n & 3
        dz = (z + k) & 3

        def piece(f, ref, at):
            if middle_first:
                dx, dy = (x + i) & 3, (y + f) & 3
            else:
                dy, dx = (y + i) & 3, (x + f) & 3
            body(ref.at[at, k], (dz * SIDE + dy) * SIDE + dx)

        piece(0, own, i)
        piece(1, above, i)
        piece(3, below, i)

        @pl.when(i < 2)
        def _():
            piece(2, low, i)

        @pl.when(i >= 2)
        def _():
            piece(2, high, i - 2)

        return 0

    lax.fori_loop(0, SIDE * SIDE, one, 0)


def place_of(where):
    d = where[0]
    return d >> 4, (d >> 2) & 3, d & 3


def sigmoid_times(value):
    return value / (1.0 + jnp.exp(-value))


def order_matrix(rows, columns, drafts, count):
    i = lax.broadcasted_iota(jnp.int32, (rows, columns), 0)
    j = lax.broadcasted_iota(jnp.int32, (rows, columns), 1)
    return ((i % count) * drafts + i // count == j).astype(BF)


def prep_kernel(h0, h1, h2, h3, normed_out, base_out, plain):
    tokens = normed_out.shape[1]
    count = 32
    blocks = (h0, h1, h2, h3)
    step = 32

    def norm(n, _):
        at = pl.ds(pl.multiple_of(n * step, step), step)
        rows = [h[at, :].astype(F32) for h in blocks]
        total = sum(jnp.sum(r * r, axis=1, keepdims=True) for r in rows)
        scale = lax.rsqrt(total / (4.0 * rows[0].shape[1]) + EPS)
        for k, h in enumerate(blocks):
            gain = h[pl.ds(tokens, 1), :].astype(F32)
            plain[k, at, :] = (rows[k] * scale * gain).astype(BF)
        return 0

    lax.fori_loop(0, tokens // step, norm, 0)
    order = order_matrix(tokens, tokens, tokens // count, count)
    base_out[...] = jnp.dot(order, h0[:tokens, :], preferred_element_type=F32).astype(BF)
    for k in range(4):
        normed_out[k] = jnp.dot(order, plain[k], preferred_element_type=F32).astype(BF)


def front_kernel(
    where, pages, accepted, normed, a0, a1, a2, a3, a4, b0, b1, b2, b3, b4,
    taps, bias, pool, inputs_out, sums_out, dt_out, pool_out,
    weight, proj, dt_raw, dt_wide, xs, edges, fresh, sems,
):
    place = place_of(where)
    m = where[1]
    drafts, count, width = xs.shape
    tokens = drafts * count
    slots = pool.shape[1]

    def take_a(src, d):
        pltpu.make_async_copy(src.at[pl.ds(0, 32), :], weight.at[pl.ds(d * 32, 32), pl.ds(0, CUT)], sems.at[0]).start()
        pltpu.make_async_copy(src.at[pl.ds(32, 16), pl.ds(0, 256)], proj.at[pl.ds(d * 16, 16), :], sems.at[1]).start()
        pltpu.make_async_copy(src.at[pl.ds(32, 16), pl.ds(256, 128)], dt_raw.at[pl.ds(d * 16, 16), :], sems.at[2]).start()

    def take_b(src, d):
        pltpu.make_async_copy(src, weight.at[pl.ds(d * 32, 32), pl.ds(CUT, width - CUT)], sems.at[0]).start()

    start_pieces((a0, a1, a2, a3, a4), place, True, take_a)
    start_pieces((b0, b1, b2, b3, b4), place, False, take_b)

    def edge(r, _):
        slot = lax.rem(pages[r], slots)
        for k in range(3):
            edges[k, pl.ds(r, 1), :] = pool[k, pl.ds(slot, 1), :]
        return 0

    lax.fori_loop(0, count, edge, 0)
    pltpu.make_async_copy(weight, weight, sems.at[0]).wait()
    pltpu.make_async_copy(proj, proj, sems.at[1]).wait()
    pltpu.make_async_copy(dt_raw, dt_raw, sems.at[2]).wait()

    def project(n, _):
        at = pl.ds(pl.multiple_of(n * 256, 256), 256)
        total = jnp.zeros((tokens, 256), F32)
        for k in range(4):
            total = total + jnp.dot(
                normed[k], weight[pl.ds((m ^ k) * 512, 512), at], preferred_element_type=F32
            )
        xs[:, :, at] = total.astype(BF).astype(F32).reshape(drafts, count, 256)
        return 0

    lax.fori_loop(0, width // 256, project, 0)

    def mix(n, _):
        rows = pl.ds(pl.multiple_of((n // 4) * 16, 16), 16)
        at = pl.ds(pl.multiple_of((n % 4) * 256, 256), 256)
        acc = jnp.concatenate([accepted[rows, :]] * 2, axis=1)
        window = [edges[k, rows, at] for k in range(3)]
        kept = [window[0], window[0], window[0]]
        for p in range(1, 3):
            for k in range(3):
                kept[k] = jnp.where(acc + k == p, window[p], kept[k])
        tap = [taps[k : k + 1, at] for k in range(4)]
        base = bias[:, at]
        for t in range(drafts):
            now = xs[t, rows, at]
            mixed = base + tap[0] * window[0]
            mixed = mixed + tap[1] * window[1]
            mixed = mixed + tap[2] * window[2]
            mixed = mixed + tap[3] * now
            inputs_out[pl.ds(pl.multiple_of(t * count + (n // 4) * 16, 16), 16), at] = sigmoid_times(mixed).astype(BF)
            for k in range(3):
                kept[k] = jnp.where(acc + k == t + 3, now, kept[k])
            window = [window[1], window[2], now]
        for k in range(3):
            fresh[k, rows, at] = kept[k]
        return 0

    lax.fori_loop(0, (count // 16) * (width // 256), mix, 0)
    sums = lax.dot_general(
        proj[...], inputs_out[...], (((0,), (1,)), ((), ())), preferred_element_type=F32
    )
    sums_out[...] = sums[: sums_out.shape[0]]
    dt_wide[...] = dt_raw[...].astype(F32)
    for c in range(width // 128):
        dt_out[:, c * 128 : (c + 1) * 128] = dt_wide[pl.ds(c, 128, stride=8), :].astype(BF)
    pool_out[...] = pool[...]

    def settle(r, _):
        slot = lax.rem(pages[r], slots)
        for k in range(3):
            pool_out[k, pl.ds(slot, 1), :] = fresh[k, pl.ds(r, 1), :]
        return 0

    lax.fori_loop(0, count, settle, 0)


def scan_kernel(
    pages, accepted, sums_a, sums_b, dt, dt_bias, a_log, inputs, pool, ys_out, kept,
    low, both, delta, decay, start, wide, pick,
):
    tokens, width = inputs.shape
    count = accepted.shape[0]
    drafts = tokens // count
    states = a_log.shape[0]
    rank = low.shape[1]
    slots = pool.shape[0] // states

    def fetch(r, _):
        slot = lax.rem(pages[r], slots)
        for c in range(width // 128):
            start[c, pl.ds(pl.multiple_of(r * states, states), states), :] = pool[
                pl.ds(pl.multiple_of(slot * states, states), states), c * 128 : (c + 1) * 128
            ]
        return 0

    lax.fori_loop(0, count, fetch, 0)
    summed = sums_a[...] + sums_b[...].astype(F32)
    low[...] = summed[:rank].T.astype(BF)
    rest = summed[rank:]
    high = rest.astype(BF).astype(F32)
    middle = (rest - high).astype(BF).astype(F32)
    parts = [high, middle, rest - high - middle, jnp.zeros_like(rest)]
    both[...] = jnp.concatenate(parts, axis=0).T
    row = lax.broadcasted_iota(jnp.int32, (128, 128), 0)
    for q in range(2 * states):
        hit = ((row & (2 * states - 1)) == q) & (row < 6 * states)
        pick[:, q * 128 : (q + 1) * 128] = hit.astype(F32).astype(BF)

    def steps(n, _):
        at = pl.ds(pl.multiple_of(n * 256, 256), 256)
        value = jnp.dot(low[...], dt[:, at], preferred_element_type=F32) + dt_bias[:, at]
        delta[:, at] = jnp.maximum(value, 0.0) + jnp.log1p(jnp.exp(-jnp.abs(value)))
        return 0

    lax.fori_loop(0, width // 256, steps, 0)
    for s in range(states):
        decay[s] = jnp.broadcast_to(-jnp.exp(a_log[s : s + 1, :]) * LOG2E, (8, width))

    def some(rb, _):
        eight = pl.ds(pl.multiple_of(rb * 8, 8), 8)
        terms = jnp.concatenate(
            [both[pl.ds(pl.multiple_of(t * count + rb * 8, 8), 8), :] for t in range(drafts)], axis=0
        ).astype(BF)
        for q in range(0, 2 * states, 4):
            spread = jnp.dot(terms, pick[:, q * 128 : (q + 4) * 128], preferred_element_type=F32)
            for p in range(4):
                wide[:, q + p] = spread[:, p * 128 : (p + 1) * 128].reshape(drafts, 8, 128)
        last = accepted[eight, :] - 1

        def columns(cp, _):
            ats = [pl.ds(pl.multiple_of(cp * 256 + h * 128, 128), 128) for h in range(2)]
            first = tuple(
                start[cp * 2 + h, pl.ds(rb * 8 * states + s, 8, stride=states), :]
                for h in range(2)
                for s in range(states)
            )

            def advance(t, state):
                rows = pl.ds(pl.multiple_of(t * count + rb * 8, 8), 8)
                d = [delta[rows, at] for at in ats]
                drive = [d[h] * inputs[rows, ats[h]].astype(F32) for h in range(2)]
                here = last == t
                out = [None, None]
                nexts = [[], []]
                for s in range(states):
                    b, c = wide[t, s], wide[t, states + s]
                    for h in range(2):
                        new = jnp.exp2(d[h] * decay[s, :, ats[h]]) * state[h * states + s] + drive[h] * b
                        term = new * c
                        out[h] = term if out[h] is None else out[h] + term
                        pltpu.store(kept.at[cp * 2 + h, pl.ds(pl.multiple_of(s * count + rb * 8, 8), 8), :], new, mask=here)
                        nexts[h].append(new)
                for h in range(2):
                    ys_out[rows, ats[h]] = out[h]
                return (*nexts[0], *nexts[1])

            lax.fori_loop(0, drafts, advance, first, unroll=4)
            return 0

        lax.fori_loop(0, width // 256, columns, 0)
        return 0

    lax.fori_loop(0, count // 8, some, 0)


def settle_kernel(pages, kept, pool, pool_out):
    chunks, rows, _ = kept.shape
    count = pages.shape[0]
    states = rows // count
    slots = pool.shape[0] // states

    def carry_over(n, _):
        at = pl.ds(pl.multiple_of(n * states, states), states)
        pool_out[at, :] = pool[at, :]
        return 0

    lax.fori_loop(0, slots, carry_over, 0)

    def settle(r, _):
        slot = lax.rem(pages[r], slots)
        for c in range(chunks):
            for s in range(0, states, 8):
                pool_out[
                    pl.ds(pl.multiple_of(slot * states + s, 8), 8), c * 128 : (c + 1) * 128
                ] = kept[c, pl.ds(s * count + r, 8, stride=count), :]
        return 0

    lax.fori_loop(0, count, settle, 0)


def gate_kernel(
    where, normed, inputs, ys, skip, second, send_out, keep_out, weight, outer, gated, sems
):
    m = where[1]
    tokens, width = gated.shape
    for z in range(SIDE):
        at = (z + SIDE - (where[0] >> 4)) & 3
        pltpu.make_async_copy(second.at[:, at, pl.ds(0, 32), :], weight.at[z], sems.at[0]).start()
    for z in range(SIDE):
        at = (z + SIDE - (where[0] >> 4)) & 3
        pltpu.make_async_copy(second.at[:, at, pl.ds(32, 32), :], outer.at[z], sems.at[1]).start()
    pltpu.make_async_copy(weight, weight, sems.at[0]).wait()

    def gate(n, _):
        at = pl.ds(pl.multiple_of(n * 256, 256), 256)
        total = jnp.zeros((tokens, 256), F32)
        for k in range(4):
            block = weight[m ^ k, :, :, at].reshape(512, 256)
            total = total + jnp.dot(normed[k], block, preferred_element_type=F32)
        gates = total.astype(BF).astype(F32)
        mixed = ys[:, at] + skip[:, at] * inputs[:, at].astype(F32)
        gated[:, at] = (mixed * sigmoid_times(gates)).astype(BF)
        return 0

    lax.fori_loop(0, width // 256, gate, 0)
    pltpu.make_async_copy(outer, outer, sems.at[1]).wait()

    def out(part, _):
        column = pl.ds(pl.multiple_of((part & 1) * 256, 256), 256)
        for core in range(2):
            block = m ^ ((part & 2) + core)
            rows = outer[block, pl.ds((part & 1) * 8, 8), :, :].reshape(256, width)
            value = lax.dot_general(
                gated[...], rows, (((1,), (1,)), ((), ())), preferred_element_type=F32
            )
            if core:
                send_out[part >> 1, :, column] = value.astype(BF)
            else:
                keep_out[part >> 1, :, column] = value
        return 0

    lax.fori_loop(0, 4, out, 0)


def join_kernel(targets, keep, near, far, base, out, total):
    tokens, width = base.shape
    count = targets.shape[0]
    drafts = tokens // count
    order = order_matrix(tokens, tokens, drafts, count)
    summed = keep[0] + near[0].astype(F32) + far[...].astype(F32)
    rounded = (summed + base[...].astype(F32)).astype(BF)
    back = lax.dot_general(order, rounded, (((0,), (0,)), ((), ())), preferred_element_type=F32)
    total[...] = back.astype(BF).reshape(count, drafts, width)
    out[...] = jnp.zeros(out.shape, BF)

    def place(r, _):
        out[lax.div(targets[r], count)] = total[r]
        return 0

    lax.fori_loop(0, count, place, 0)


def unpack_kernel(where, targets, got, out):
    count = targets.shape[0]
    peers = got.shape[0]

    def take(r, _):
        source = lax.rem(2 * where[0] - lax.div(targets[r], count) + 2 * peers, peers)
        out[r] = got[source]
        return 0

    lax.fori_loop(0, count, take, 0)


def params():
    return pltpu.CompilerParams(vmem_limit_bytes=56 << 20)


def on_device(
    hidden, norm_gain, in_x, in_z, conv_weight, conv_bias, x_proj, dt_proj, dt_bias, a_log, skip,
    out_proj, state_pool, conv_pool, permutation, page_table, accepted,
):
    count, drafts, part = hidden.shape
    tokens = count * drafts
    width = in_x.shape[1]
    slots, states, _ = state_pool.shape
    rank = x_proj.shape[1] - 2 * states
    where = jnp.stack([lax.axis_index("dp"), lax.axis_index("mp")]).astype(jnp.int32)
    peers = lax.axis_size("dp")

    extra = jnp.concatenate(
        [
            x_proj,
            jnp.zeros((16, 256 - x_proj.shape[1]), BF),
            dt_proj.reshape(16, 128),
            jnp.zeros((16, width - CUT), BF),
        ],
        axis=1,
    )
    first = direct(jnp.concatenate([in_x, extra], axis=0), 0)
    middle_a = direct(first[:, :, :CUT], 2)
    middle_b = direct(first[:, :32, CUT:], 1)
    middle_a, middle_b = lax.optimization_barrier((middle_a, middle_b))
    sides_a, sides_b = ring_one(middle_a, 1), ring_one(middle_b, 2)
    first_a = ring_two(middle_a, 1, sides_a)
    first_b = ring_two(middle_b, 2, sides_b)

    flat = hidden.reshape(tokens, part)
    sent = jnp.concatenate([flat, jnp.broadcast_to(norm_gain[None], (16, part))], axis=0)
    sent = after(sent, middle_a, middle_b)
    near = across(sent, 1)
    far = across(sent, 2)
    both = across(far, 1)
    normed, base = pl.pallas_call(
        prep_kernel,
        out_shape=(
            jax.ShapeDtypeStruct((4, tokens, part), BF),
            jax.ShapeDtypeStruct((tokens, part), BF),
        ),
        in_specs=[VMEM] * 4,
        out_specs=(VMEM,) * 2,
        scratch_shapes=[pltpu.VMEM((4, tokens, part), BF)],
        compiler_params=params(),
        cost_estimate=pl.CostEstimate(flops=1_000_000, bytes_accessed=1 << 10, transcendentals=0),
        name="prep",
    )(sent, *after((near, far, both), sides_a, sides_b))

    pair = after(jnp.concatenate([in_z, out_proj.T], axis=0), first)
    second = lax.all_gather(
        jnp.stack(after(send_direct(pair, 0), middle_a, middle_b)), "dp", axis=0,
        axis_index_groups=[[z * 16 + i for i in range(16)] for z in range(SIDE)],
    )

    wide_accepted = jnp.broadcast_to(accepted[:, None], (count, 128))
    inputs, sums, dt, new_conv = pl.pallas_call(
        front_kernel,
        out_shape=(
            jax.ShapeDtypeStruct((tokens, width), BF),
            jax.ShapeDtypeStruct((rank + 2 * states, tokens), F32),
            jax.ShapeDtypeStruct((rank, width), BF),
            jax.ShapeDtypeStruct((3, slots, width), F32),
        ),
        in_specs=[SMEM, SMEM] + [VMEM] * 2 + [ANY] * 10 + [VMEM] * 3,
        out_specs=(VMEM,) * 4,
        scratch_shapes=[
            pltpu.VMEM((2048, width), BF),
            pltpu.VMEM((1024, 256), BF),
            pltpu.VMEM((1024, 128), BF),
            pltpu.VMEM((1024, 128), F32),
            pltpu.VMEM((drafts, count, width), F32),
            pltpu.VMEM((3, count, width), F32),
            pltpu.VMEM((3, count, width), F32),
            pltpu.SemaphoreType.DMA((3,)),
        ],
        compiler_params=params(),
        cost_estimate=pl.CostEstimate(flops=12_000_000_000, bytes_accessed=1 << 10, transcendentals=0),
        name="front",
    )(
        where, page_table, wide_accepted, normed, *first_a, *first_b,
        conv_weight, conv_bias[None], conv_pool.transpose(1, 0, 2),
    )

    sums = sums + across(sums, 1)
    other = across(sums.astype(BF), 2)
    ys, kept = pl.pallas_call(
        scan_kernel,
        out_shape=(
            jax.ShapeDtypeStruct((tokens, width), F32),
            jax.ShapeDtypeStruct((width // 128, states * count, 128), F32),
        ),
        in_specs=[SMEM] + [VMEM] * 8,
        out_specs=(VMEM,) * 2,
        scratch_shapes=[
            pltpu.VMEM((tokens, rank), BF),
            pltpu.VMEM((tokens, 128), F32),
            pltpu.VMEM((tokens, width), F32),
            pltpu.VMEM((states, 8, width), F32),
            pltpu.VMEM((width // 128, count * states, 128), F32),
            pltpu.VMEM((drafts, 2 * states, 8, 128), F32),
            pltpu.VMEM((128, 2 * states * 128), BF),
        ],
        compiler_params=params(),
        cost_estimate=pl.CostEstimate(flops=1_000_000, bytes_accessed=1 << 10, transcendentals=0),
        name="scan",
    )(
        page_table, wide_accepted, sums, other, dt, dt_bias[None], a_log, inputs,
        state_pool.reshape(slots * states, width),
    )

    new_state = pl.pallas_call(
        settle_kernel,
        out_shape=jax.ShapeDtypeStruct((slots * states, width), F32),
        in_specs=[SMEM, VMEM, VMEM],
        out_specs=VMEM,
        compiler_params=params(),
        cost_estimate=pl.CostEstimate(flops=1_000_000, bytes_accessed=1 << 10, transcendentals=0),
        name="settle",
    )(page_table, kept, state_pool.reshape(slots * states, width))

    send, keep = pl.pallas_call(
        gate_kernel,
        out_shape=(
            jax.ShapeDtypeStruct((2, tokens, part), BF),
            jax.ShapeDtypeStruct((2, tokens, part), F32),
        ),
        in_specs=[SMEM] + [VMEM] * 4 + [ANY],
        out_specs=(VMEM,) * 2,
        scratch_shapes=[
            pltpu.VMEM((SIDE, 16, 32, width), BF),
            pltpu.VMEM((SIDE, 16, 32, width), BF),
            pltpu.VMEM((tokens, width), BF),
            pltpu.SemaphoreType.DMA((2,)),
        ],
        compiler_params=params(),
        cost_estimate=pl.CostEstimate(flops=1_000_000, bytes_accessed=1 << 10, transcendentals=0),
        name="gate",
    )(where, normed, inputs, ys, skip[None], second)
    got = across(send, 1)
    remote = across((keep[1] + got[1].astype(F32)).astype(BF), 2)
    packed = pl.pallas_call(
        join_kernel,
        out_shape=jax.ShapeDtypeStruct((peers, drafts, part), BF),
        in_specs=[SMEM] + [VMEM] * 4,
        out_specs=VMEM,
        scratch_shapes=[pltpu.VMEM((count, drafts, part), BF)],
        compiler_params=params(),
        cost_estimate=pl.CostEstimate(flops=1_000_000, bytes_accessed=1 << 10, transcendentals=0),
        name="join",
    )(permutation, keep, got, remote, base)
    arrived = lax.all_to_all(packed, "dp", split_axis=0, concat_axis=0, tiled=True)
    verified = pl.pallas_call(
        unpack_kernel,
        out_shape=jax.ShapeDtypeStruct((count, drafts, part), BF),
        in_specs=[SMEM, SMEM, VMEM],
        out_specs=VMEM,
        name="unpack",
    )(where, permutation, arrived)
    return (
        verified,
        new_state.reshape(slots, states, width),
        new_conv.transpose(1, 0, 2),
    )


def solution(mesh):
    return jax.shard_map(
        on_device,
        mesh=mesh,
        in_specs=(
            P("dp", None, "mp"),
            P("mp"),
            P("dp", "mp"),
            P("dp", "mp"),
            P(None, "mp"),
            P("mp"),
            P(("mp", "dp"), None),
            P("dp", "mp"),
            P("mp"),
            P(None, "mp"),
            P("mp"),
            P("mp", "dp"),
            P("dp", None, "mp"),
            P("dp", None, "mp"),
            P("dp"),
            P("dp"),
            P("dp"),
        ),
        out_specs=(P("dp", None, "mp"), P("dp", None, "mp"), P("dp", None, "mp")),
        check_vma=False,
    )
```
